32 devices in a mesh: dp: 4 (over z), ctx: 2 (over x), fsdp: 4 (over y, core).
Axes of the slice: x: 2, y: 2, z: 4, core: 2. Of those that a mesh axis runs over, the one named last changes fastest.
Arguments:
- tokens: bfloat16 [16, 256, 1536], P(('dp', 'fsdp'), 'ctx'), may hold values from -6 to 6
- cotangent: bfloat16 [16, 256, 1536], P(('dp', 'fsdp'), 'ctx'), may hold values from -6 to 6
- rope_positions: int32 [16, 256], P('dp', 'ctx'), may hold values from 0 to 383, as said below
- block_order: int32 [4], replicated, may hold values from 0 to 3, as said below
- w_query: bfloat16 [1536, 1536], P('fsdp'), may hold values from -0.15625 to 0.15625
- key_weight: bfloat16 [1536, 768], P('fsdp'), may hold values from -0.15625 to 0.15625
- value_weight: bfloat16 [1536, 768], P('fsdp'), may hold values from -0.15625 to 0.15625
- w_out: bfloat16 [1536, 1536], P('fsdp'), may hold values from -3 to 3
- w_gate: bfloat16 [1536, 4096], P('fsdp'), may hold values from -0.15625 to 0.15625
- w_up: bfloat16 [1536, 4096], P('fsdp'), may hold values from -0.15625 to 0.15625
- w_down: bfloat16 [4096, 1536], P('fsdp'), may hold values from -0.09375 to 0.09375
- attn_gain: bfloat16 [1536], P('fsdp'), as said below
- mlp_gain: bfloat16 [1536], P('fsdp'), may hold values from 0.25 to 1.75
Outputs:
- output: bfloat16 [16, 256, 1536], P(('dp', 'fsdp'), 'ctx')
- grad_tokens: bfloat16 [16, 256, 1536], P(('dp', 'fsdp'), 'ctx')
- grad_query: float32 [1536, 1536], P(('dp', 'ctx'), 'fsdp')
- grad_key: float32 [1536, 768], P(('dp', 'ctx'), 'fsdp')
- grad_value: float32 [1536, 768], P(('dp', 'ctx'), 'fsdp')
- grad_outproj: float32 [1536, 1536], P('fsdp', ('dp', 'ctx'))
- grad_gate: float32 [1536, 4096], P(('dp', 'ctx'), 'fsdp')
- grad_up: float32 [1536, 4096], P(('dp', 'ctx'), 'fsdp')
- grad_down: float32 [4096, 1536], P('fsdp', ('dp', 'ctx'))
- grad_attn_gain: float32 [1536], P(('dp', 'ctx', 'fsdp'))
- grad_mlp_gain: float32 [1536], P(('dp', 'ctx', 'fsdp'))
The draws below stay inside these ranges and needn't reach their ends.
Inputs may be any that keep to these rules, and one draw needn't show every extreme that they name: block_order holds every block number once; dealt blocks 2c and 2c + 1 are a mirrored pair j and 3 - j. `rope_positions`: taken in the token order that block_order gives, positions of a sequence start at 0 and rise from token to token by 2 at exactly 128 steps and by 1 at the others, so the last token of every sequence has the largest position. `attn_gain`: positive gains.
All inputs are finite; a program needn't handle non-finite values.
Results may differ from the reference program's by a relative error of at most 0.025.
Values may be sent and summed in bfloat16 or wider, within the bound.
No kernel may reach another device: no remote copies, remote signals or barrier semaphores. Data moves between devices by JAX's collectives and lax.ppermute only.
A program may use at most 320 MiB of HBM per device.

```python
import jax
import jax.numpy as jnp
from jax import lax

MODEL_WIDTH = 1536
QUERY_HEADS = 16
KEY_VALUE_HEADS = 8
HEAD_SIZE = 96
FF = 4096
BLK = 64
NBLK = 4
SEQUENCE_TOKENS = 256
SEQS = 16


def deal_order(key):
    pair_count = NBLK // 2
    paired = jax.random.permutation(jax.random.fold_in(key, 11), pair_count).astype(jnp.int32)
    flipped = jax.random.randint(jax.random.fold_in(key, 12), (pair_count,), 0, 2)
    first_block = jnp.where(flipped == 1, NBLK - 1 - paired, paired)
    second_block = NBLK - 1 - first_block
    return jnp.stack([first_block, second_block], axis=1).reshape(-1).astype(jnp.int32)


def draw_block_order(key, part):
    return deal_order(key)


def draw_rope_positions(key, part):
    step_pattern = jnp.where(jnp.arange(SEQUENCE_TOKENS - 1, dtype=jnp.int32) < SEQUENCE_TOKENS // 2, 2, 1).astype(jnp.int32)
    seq_keys = jax.random.split(jax.random.fold_in(key, 13), SEQS)
    increments = jax.vmap(lambda one_key: jax.random.permutation(one_key, step_pattern))(seq_keys).astype(jnp.int32)
    natural = jnp.concatenate([jnp.zeros((SEQS, 1), jnp.int32), jnp.cumsum(increments, axis=1).astype(jnp.int32)], axis=1)
    dealt = deal_order(key)
    row_source = (dealt[:, None] * BLK + jnp.arange(BLK, dtype=jnp.int32)[None, :]).reshape(-1)
    return jnp.take(natural, row_source, axis=1).astype(jnp.int32)


def draw_attn_gain(key, part):
    gains = jax.random.uniform(key, (MODEL_WIDTH,), jnp.float32, 0.6, 1.4)
    return gains.astype(jnp.bfloat16)


def block_scale(own_key, extent, cuts, least, top_value):
    factor_of = 1.0
    for position, blocks in cuts:
        draws = jax.random.uniform(jax.random.fold_in(jax.random.fold_in(own_key, 6), position), (blocks,), jnp.float32, least / len(cuts), top_value / len(cuts))
        factor_of = factor_of * jnp.repeat(jnp.exp(draws), extent[position] // blocks).reshape((-1,) + (1,) * (len(extent) - 1 - position))
    return factor_of


def bell_draw(own_key, dims, deviation, reach, cuts=(), kind=jnp.bfloat16):
    result = deviation * jax.random.normal(own_key, dims, jnp.float32)
    if cuts:
        result = result * block_scale(own_key, dims, cuts, -0.22, 0.18)
    return jnp.clip(result, -reach, reach).astype(kind)


def setup_inputs(seed: int = 0) -> dict:
    keys = jax.random.split(jax.random.key(seed), 14)
    return {
        "tokens": bell_draw(keys[0], (SEQS, SEQUENCE_TOKENS, MODEL_WIDTH), 1.0, 6.0, ((0, 16), (1, 2))),
        "cotangent": bell_draw(keys[1], (SEQS, SEQUENCE_TOKENS, MODEL_WIDTH), 1.0, 6.0, ((0, 16), (1, 2))),
        "rope_positions": draw_rope_positions(jax.random.fold_in(keys[13], 71), 0),
        "block_order": draw_block_order(jax.random.fold_in(keys[13], 71), 0),
        "w_query": bell_draw(keys[4], (MODEL_WIDTH, QUERY_HEADS * HEAD_SIZE), MODEL_WIDTH ** -0.5, 0.15625, ((0, 4),)),
        "key_weight": bell_draw(keys[5], (MODEL_WIDTH, KEY_VALUE_HEADS * HEAD_SIZE), MODEL_WIDTH ** -0.5, 0.15625, ((0, 4),)),
        "value_weight": bell_draw(keys[6], (MODEL_WIDTH, KEY_VALUE_HEADS * HEAD_SIZE), MODEL_WIDTH ** -0.5, 0.15625, ((0, 4),)),
        "w_out": bell_draw(keys[7], (QUERY_HEADS * HEAD_SIZE, MODEL_WIDTH), 4 ** -0.5, 3.0, ((0, 4),)),
        "w_gate": bell_draw(keys[8], (MODEL_WIDTH, FF), MODEL_WIDTH ** -0.5, 0.15625, ((0, 4),)),
        "w_up": bell_draw(keys[9], (MODEL_WIDTH, FF), MODEL_WIDTH ** -0.5, 0.15625, ((0, 4),)),
        "w_down": bell_draw(keys[10], (FF, MODEL_WIDTH), FF ** -0.5, 0.09375, ((0, 4),)),
        "attn_gain": draw_attn_gain(jax.random.fold_in(keys[13], 71), 0),
        "mlp_gain": jnp.clip(1.0 + 0.15 * jax.random.normal(keys[12], (MODEL_WIDTH,), jnp.float32), 0.25, 1.75).astype(jnp.bfloat16),
    }


rope_base = 100000.0
norm_eps = 1e-05
masked_score = -1e+30

def matrix_product(left, right):
    return jnp.dot(left, right, preferred_element_type=jnp.float32)

def rounded(values):
    return lax.optimization_barrier(values.astype(jnp.bfloat16)).astype(jnp.float32)

def rope_tables(positions):
    half_dim = HEAD_SIZE // 2
    inverse = rope_base ** (-2.0 * jnp.arange(half_dim, dtype=jnp.float32) / HEAD_SIZE)
    angles = positions.astype(jnp.float32)[:, None] * inverse[None, :]
    return (jnp.cos(angles), jnp.sin(angles))

def apply_rotary(values, cosine_table, sine_table, head_count, direction):
    count_of_rows = values.shape[0]
    half_dim = HEAD_SIZE // 2
    halves = values.reshape(count_of_rows, head_count, 2, half_dim)
    first_half = halves[:, :, 0, :]
    second_half = halves[:, :, 1, :]
    cos_part = cosine_table[:, None, :]
    sin_part = direction * sine_table[:, None, :]
    joined = jnp.stack([first_half * cos_part - second_half * sin_part, second_half * cos_part + first_half * sin_part], axis=2)
    return joined.reshape(count_of_rows, head_count * HEAD_SIZE)

def normalize(values):
    inv_root = lax.rsqrt(lax.optimization_barrier(jnp.mean(values * values, axis=-1, keepdims=True)) + norm_eps)
    return (values * inv_root, inv_root)

def norm_back(grad_output, unit_rows, inv_root, gain_vec):
    grad_unit = grad_output * gain_vec
    grad_gain = lax.optimization_barrier(jnp.sum(grad_output * unit_rows, axis=0))
    grad_input = inv_root * (grad_unit - unit_rows * lax.optimization_barrier(jnp.mean(grad_unit * unit_rows, axis=-1, keepdims=True)))
    return (grad_input, grad_gain)

def token_index(block_order):
    return (block_order[:, None] * BLK + jnp.arange(BLK, dtype=jnp.int32)[None, :]).reshape(-1).astype(jnp.int32)

def masked_scores(head_queries, head_keys, query_tokens, key_tokens):
    scores = jnp.einsum('qngd,knd->ngqk', head_queries, head_keys) * HEAD_SIZE ** (-0.5)
    allowed = key_tokens[None, None, None, :] <= query_tokens[None, None, :, None]
    return (jnp.where(allowed, scores, masked_score), allowed)

def attend_forward(query_matrix, rotated_keys, every_value, query_tokens, key_tokens):
    count_of_rows = query_matrix.shape[0]
    query_group_width = QUERY_HEADS // KEY_VALUE_HEADS
    head_queries = query_matrix.astype(jnp.float32).reshape(count_of_rows, KEY_VALUE_HEADS, query_group_width, HEAD_SIZE)
    head_keys = rotated_keys.astype(jnp.float32).reshape(-1, KEY_VALUE_HEADS, HEAD_SIZE)
    head_values = every_value.astype(jnp.float32).reshape(-1, KEY_VALUE_HEADS, HEAD_SIZE)
    scores, allowed = masked_scores(head_queries, head_keys, query_tokens, key_tokens)
    row_max = lax.optimization_barrier(jnp.max(scores, axis=-1))
    row_sum = lax.optimization_barrier(jnp.sum(jnp.where(allowed, jnp.exp(scores - row_max[..., None]), 0.0), axis=-1))
    log_sums = row_max + jnp.log(row_sum)
    attn_prob = rounded(jnp.where(allowed, jnp.exp(scores - log_sums[..., None]), 0.0))
    mixed = jnp.einsum('ngqk,knd->qngd', attn_prob, head_values)
    return (mixed.reshape(count_of_rows, QUERY_HEADS * HEAD_SIZE).astype(jnp.bfloat16), log_sums)

def attend_backward(query_matrix, attended_gradient, attended_output, log_sums, query_tokens, rotated_keys, every_value, key_tokens):
    count_of_rows = query_matrix.shape[0]
    query_group_width = QUERY_HEADS // KEY_VALUE_HEADS
    head_queries = query_matrix.astype(jnp.float32).reshape(count_of_rows, KEY_VALUE_HEADS, query_group_width, HEAD_SIZE)
    head_gradient = attended_gradient.astype(jnp.float32).reshape(count_of_rows, KEY_VALUE_HEADS, query_group_width, HEAD_SIZE)
    head_outputs = attended_output.astype(jnp.float32).reshape(count_of_rows, KEY_VALUE_HEADS, query_group_width, HEAD_SIZE)
    head_keys = rotated_keys.astype(jnp.float32).reshape(-1, KEY_VALUE_HEADS, HEAD_SIZE)
    head_values = every_value.astype(jnp.float32).reshape(-1, KEY_VALUE_HEADS, HEAD_SIZE)
    scores, allowed = masked_scores(head_queries, head_keys, query_tokens, key_tokens)
    attn_prob = jnp.where(allowed, jnp.exp(scores - log_sums[..., None]), 0.0)
    row_delta = jnp.transpose(lax.optimization_barrier(jnp.sum(head_gradient * head_outputs, axis=-1)), (1, 2, 0))
    grad_prob = jnp.einsum('qngd,knd->ngqk', head_gradient, head_values)
    grad_scores = rounded(attn_prob * (grad_prob - row_delta[..., None]) * HEAD_SIZE ** (-0.5))
    value_gradient = jnp.einsum('ngqk,qngd->knd', rounded(attn_prob), head_gradient)
    key_gradient = jnp.einsum('ngqk,qngd->knd', grad_scores, head_queries)
    grad_queries = jnp.einsum('ngqk,knd->qngd', grad_scores, head_keys).reshape(count_of_rows, QUERY_HEADS * HEAD_SIZE)
    return (grad_queries, key_gradient, value_gradient)

def reference(tokens, cotangent, rope_positions, block_order, w_query, key_weight, value_weight, w_out, w_gate, w_up, w_down, attn_gain, mlp_gain):
    key_tokens = token_index(block_order)
    block_rows = 2 * BLK
    query_blocks = SEQUENCE_TOKENS // block_rows
    first_gain = attn_gain.astype(jnp.float32)
    second_gain = mlp_gain.astype(jnp.float32)

    def per_sequence(sums, sequence):
        inputs, grad_out, positions = sequence
        residual_in = inputs.astype(jnp.float32)
        unit_first, root_first = normalize(residual_in)
        first_normed_input = (unit_first * first_gain).astype(jnp.bfloat16)
        cosine_table, sine_table = rope_tables(positions)
        query_matrix = apply_rotary(matrix_product(first_normed_input, w_query), cosine_table, sine_table, QUERY_HEADS, 1.0).astype(jnp.bfloat16)
        rotated_keys = apply_rotary(matrix_product(first_normed_input, key_weight), cosine_table, sine_table, KEY_VALUE_HEADS, 1.0).astype(jnp.bfloat16)
        every_value = matrix_product(first_normed_input, value_weight).astype(jnp.bfloat16)
        query_split = query_matrix.reshape(query_blocks, block_rows, QUERY_HEADS * HEAD_SIZE)
        token_split = key_tokens.reshape(query_blocks, block_rows)

        def forward_block(block_in):
            return attend_forward(block_in[0], rotated_keys, every_value, block_in[1], key_tokens)
        attended_split, log_sums = lax.map(forward_block, (query_split, token_split))
        attended_output = attended_split.reshape(SEQUENCE_TOKENS, QUERY_HEADS * HEAD_SIZE)
        hidden_res = residual_in + matrix_product(attended_output, w_out)
        unit_second, root_second = normalize(hidden_res)
        normed_second = (unit_second * second_gain).astype(jnp.bfloat16)
        gate_pre = matrix_product(normed_second, w_gate)
        up_pre = matrix_product(normed_second, w_up)
        sigmoid_gate = jax.nn.sigmoid(gate_pre)
        silu_gate = gate_pre * sigmoid_gate
        activated = (silu_gate * up_pre).astype(jnp.bfloat16)
        output = (hidden_res + matrix_product(activated, w_down)).astype(jnp.bfloat16)
        grad_down = matrix_product(activated.T, grad_out)
        grad_act = matrix_product(grad_out, w_down.T)
        grad_gate_pre = (grad_act * up_pre * sigmoid_gate * (1.0 + gate_pre * (1.0 - sigmoid_gate))).astype(jnp.bfloat16)
        grad_up_pre = (grad_act * silu_gate).astype(jnp.bfloat16)
        grad_gate = matrix_product(normed_second.T, grad_gate_pre)
        grad_up = matrix_product(normed_second.T, grad_up_pre)
        grad_normed = matrix_product(grad_gate_pre, w_gate.T) + matrix_product(grad_up_pre, w_up.T)
        grad_hidden, grad_second_gain = norm_back(grad_normed, unit_second, root_second, second_gain)
        grad_hidden = grad_hidden + grad_out.astype(jnp.float32)
        grad_hidden_b = grad_hidden.astype(jnp.bfloat16)
        grad_outproj = matrix_product(attended_output.T, grad_hidden_b)
        attended_gradient = matrix_product(grad_hidden_b, w_out.T).astype(jnp.bfloat16)
        grad_split = attended_gradient.reshape(query_blocks, block_rows, QUERY_HEADS * HEAD_SIZE)

        def backward_block(carried, block_in):
            query_rows, grad_rows, attended_rows, lse_rows, token_rows = block_in
            grad_queries, key_gradient, value_gradient = attend_backward(query_rows, grad_rows, attended_rows, lse_rows, token_rows, rotated_keys, every_value, key_tokens)
            return ((carried[0] + key_gradient, carried[1] + value_gradient), grad_queries)
        empty_key_value = jnp.zeros((SEQUENCE_TOKENS, KEY_VALUE_HEADS, HEAD_SIZE), jnp.float32)
        (key_gradient, value_gradient), grad_queries = lax.scan(backward_block, (empty_key_value, empty_key_value), (query_split, grad_split, attended_split, log_sums, token_split))
        grad_queries = apply_rotary(grad_queries.reshape(SEQUENCE_TOKENS, QUERY_HEADS * HEAD_SIZE), cosine_table, sine_table, QUERY_HEADS, -1.0).astype(jnp.bfloat16)
        key_gradient_b = apply_rotary(key_gradient.reshape(SEQUENCE_TOKENS, KEY_VALUE_HEADS * HEAD_SIZE), cosine_table, sine_table, KEY_VALUE_HEADS, -1.0).astype(jnp.bfloat16)
        value_gradient_b = value_gradient.reshape(SEQUENCE_TOKENS, KEY_VALUE_HEADS * HEAD_SIZE).astype(jnp.bfloat16)
        grad_wq = matrix_product(first_normed_input.T, grad_queries)
        grad_wk = matrix_product(first_normed_input.T, key_gradient_b)
        grad_wv = matrix_product(first_normed_input.T, value_gradient_b)
        grad_normed_first = matrix_product(grad_queries, w_query.T) + matrix_product(key_gradient_b, key_weight.T) + matrix_product(value_gradient_b, value_weight.T)
        grad_input, grad_first_gain = norm_back(grad_normed_first, unit_first, root_first, first_gain)
        grad_input = (grad_hidden + grad_input).astype(jnp.bfloat16)
        new_terms = (grad_wq, grad_wk, grad_wv, grad_outproj, grad_gate, grad_up, grad_down, grad_first_gain, grad_second_gain)
        updated = tuple((running_total + new_term for running_total, new_term in zip(sums, new_terms)))
        return (updated, (output, grad_input))
    params = (w_query, key_weight, value_weight, w_out, w_gate, w_up, w_down, attn_gain, mlp_gain)
    zero_sums = tuple((jnp.zeros(param_array.shape, jnp.float32) for param_array in params))
    sums, (output, grad_tokens) = lax.scan(per_sequence, zero_sums, (tokens, cotangent, rope_positions))
    return (output, grad_tokens, sums[0], sums[1], sums[2], sums[3], sums[4], sums[5], sums[6], sums[7], sums[8])
```

```python
import jax
import jax.numpy as jnp
from jax import lax
from jax.sharding import PartitionSpec as P

QUERY_HEADS = 16
KEY_VALUE_HEADS = 8
HEAD_SIZE = 96


rope_base = 100000.0
norm_eps = 1e-05
masked_score = -1e30


def matrix_product(left, right):
    return jnp.dot(left, right, preferred_element_type=jnp.float32)


def back_mul(left, right):
    return lax.dot_general(
        left, right, (((left.ndim - 1,), (1,)), ((), ())), preferred_element_type=jnp.float32
    )


def weight_term(left, right):
    return lax.dot_general(
        left, right, (((0, 1), (0, 1)), ((), ())), preferred_element_type=jnp.float32
    )


def rope_tables(positions):
    half_dim = HEAD_SIZE // 2
    inverse = rope_base ** (-2.0 * jnp.arange(half_dim, dtype=jnp.float32) / HEAD_SIZE)
    angles = positions.astype(jnp.float32)[..., None] * inverse
    return (jnp.cos(angles), jnp.sin(angles))


def apply_rotary(values, cosine_table, sine_table, direction):
    leading = values.shape[:-1]
    head_count = values.shape[-1] // HEAD_SIZE
    half_dim = HEAD_SIZE // 2
    halves = values.reshape(leading + (head_count, 2, half_dim))
    first_half = halves[..., 0, :]
    second_half = halves[..., 1, :]
    cos_part = cosine_table[..., None, :]
    sin_part = direction * sine_table[..., None, :]
    joined = jnp.stack(
        [
            first_half * cos_part - second_half * sin_part,
            second_half * cos_part + first_half * sin_part,
        ],
        axis=-2,
    )
    return joined.reshape(leading + (head_count * HEAD_SIZE,))


def normalize(values):
    inv_root = lax.rsqrt(jnp.mean(values * values, axis=-1, keepdims=True) + norm_eps)
    return (values * inv_root, inv_root)


def norm_back(grad_output, unit_rows, inv_root, gain_vec):
    grad_unit = grad_output * gain_vec
    grad_gain = jnp.sum(grad_output * unit_rows, axis=0)
    grad_input = inv_root * (
        grad_unit - unit_rows * jnp.mean(grad_unit * unit_rows, axis=-1, keepdims=True)
    )
    return (grad_input, grad_gain)


def token_lookup(block_order, row_ids, block_size, local_rows):
    slot_ids = 2 * (row_ids // local_rows) + row_ids % local_rows // block_size
    onehot_table = (
        slot_ids[:, None] == jnp.arange(block_order.shape[0], dtype=jnp.int32)[None, :]
    ).astype(jnp.int32)
    chosen = jnp.sum(onehot_table * block_order[None, :], axis=1)
    return chosen * block_size + row_ids % block_size


def attend_forward(query_matrix, key_stack, value_stack, own_tokens, token_stack):
    seq_count = query_matrix.shape[0]
    count_of_rows = query_matrix.shape[1]
    kv_heads = key_stack.shape[-1] // HEAD_SIZE
    query_group_width = QUERY_HEADS // KEY_VALUE_HEADS
    score_scale = HEAD_SIZE ** (-0.5)
    head_queries = query_matrix.reshape(
        seq_count, count_of_rows, kv_heads, query_group_width, HEAD_SIZE
    )

    def absorb(state, block_in):
        running_max, running_sum, weighted = state
        piece_keys, piece_values, piece_tokens = block_in
        piece_rows = piece_keys.shape[1]
        scores = (
            jnp.einsum(
                "sqngd,sknd->sngqk",
                head_queries,
                piece_keys.reshape(seq_count, piece_rows, kv_heads, HEAD_SIZE),
                preferred_element_type=jnp.float32,
            )
            * score_scale
        )
        allowed = piece_tokens[None, None, None, None, :] <= own_tokens[None, None, None, :, None]
        scores = jnp.where(allowed, scores, masked_score)
        new_max = jnp.maximum(running_max, jnp.max(scores, axis=-1))
        weights_now = jnp.where(allowed, jnp.exp(scores - new_max[..., None]), 0.0)
        decay_factor = jnp.exp(running_max - new_max)
        new_sum = running_sum * decay_factor + jnp.sum(weights_now, axis=-1)
        block_sum = jnp.einsum(
            "sngqk,sknd->sngqd",
            weights_now.astype(jnp.bfloat16),
            piece_values.reshape(seq_count, piece_rows, kv_heads, HEAD_SIZE),
            preferred_element_type=jnp.float32,
        )
        return ((new_max, new_sum, weighted * decay_factor[..., None] + block_sum), 0)

    stat_shape = (seq_count, kv_heads, query_group_width, count_of_rows)
    start_state = (
        jnp.full(stat_shape, masked_score, jnp.float32),
        jnp.zeros(stat_shape, jnp.float32),
        jnp.zeros(stat_shape + (HEAD_SIZE,), jnp.float32),
    )
    (running_max, running_sum, weighted), unused = lax.scan(
        absorb, start_state, (key_stack, value_stack, token_stack)
    )
    attended_output = (
        jnp.transpose(weighted / running_sum[..., None], (0, 3, 1, 2, 4))
        .reshape(seq_count, count_of_rows, kv_heads * query_group_width * HEAD_SIZE)
        .astype(jnp.bfloat16)
    )
    return (attended_output, running_max + jnp.log(running_sum))


def attend_backward(
    query_matrix,
    attended_gradient,
    attended_output,
    log_sums,
    own_tokens,
    key_stack,
    value_stack,
    token_stack,
):
    seq_count = query_matrix.shape[0]
    count_of_rows = query_matrix.shape[1]
    kv_heads = key_stack.shape[-1] // HEAD_SIZE
    query_group_width = QUERY_HEADS // KEY_VALUE_HEADS
    score_scale = HEAD_SIZE ** (-0.5)
    head_queries = query_matrix.reshape(
        seq_count, count_of_rows, kv_heads, query_group_width, HEAD_SIZE
    )
    head_gradient = attended_gradient.reshape(
        seq_count, count_of_rows, kv_heads, query_group_width, HEAD_SIZE
    )
    head_outputs = attended_output.astype(jnp.float32).reshape(
        seq_count, count_of_rows, kv_heads, query_group_width, HEAD_SIZE
    )
    row_delta = jnp.transpose(
        jnp.sum(head_gradient.astype(jnp.float32) * head_outputs, axis=-1), (0, 2, 3, 1)
    )

    def key_step(grad_query_sum, block_in):
        piece_keys, piece_values, piece_tokens = block_in
        piece_rows = piece_keys.shape[1]
        head_keys = piece_keys.reshape(seq_count, piece_rows, kv_heads, HEAD_SIZE)
        head_values = piece_values.reshape(seq_count, piece_rows, kv_heads, HEAD_SIZE)
        scores = (
            jnp.einsum(
                "sqngd,sknd->sngqk", head_queries, head_keys, preferred_element_type=jnp.float32
            )
            * score_scale
        )
        allowed = piece_tokens[None, None, None, None, :] <= own_tokens[None, None, None, :, None]
        scores = jnp.where(allowed, scores, masked_score)
        attn_prob = jnp.where(allowed, jnp.exp(scores - log_sums[..., None]), 0.0)
        grad_prob = jnp.einsum(
            "sqngd,sknd->sngqk", head_gradient, head_values, preferred_element_type=jnp.float32
        )
        grad_scores = (attn_prob * (grad_prob - row_delta[..., None]) * score_scale).astype(
            jnp.bfloat16
        )
        grad_value_piece = jnp.einsum(
            "sngqk,sqngd->sknd",
            attn_prob.astype(jnp.bfloat16),
            head_gradient,
            preferred_element_type=jnp.float32,
        )
        grad_key_piece = jnp.einsum(
            "sngqk,sqngd->sknd", grad_scores, head_queries, preferred_element_type=jnp.float32
        )
        grad_query_sum = grad_query_sum + jnp.einsum(
            "sngqk,sknd->sqngd", grad_scores, head_keys, preferred_element_type=jnp.float32
        )
        return (
            grad_query_sum,
            (
                grad_key_piece.reshape(seq_count, piece_rows, kv_heads * HEAD_SIZE),
                grad_value_piece.reshape(seq_count, piece_rows, kv_heads * HEAD_SIZE),
            ),
        )

    zero_query = jnp.zeros(
        (seq_count, count_of_rows, kv_heads, query_group_width, HEAD_SIZE), jnp.float32
    )
    grad_query_sum, (key_pieces, value_pieces) = lax.scan(
        key_step, zero_query, (key_stack, value_stack, token_stack)
    )
    return (
        grad_query_sum.reshape(seq_count, count_of_rows, kv_heads * query_group_width * HEAD_SIZE),
        key_pieces,
        value_pieces,
    )


def per_device(
    tokens,
    cotangent,
    rope_positions,
    block_order,
    w_query,
    key_weight,
    value_weight,
    w_out,
    w_gate,
    w_up,
    w_down,
    attn_gain,
    mlp_gain,
):
    local_rows = tokens.shape[1]
    block_size = local_rows // 2
    ctx_count = lax.axis_size("ctx")
    ctx_rank = lax.axis_index("ctx")
    shard_rank = lax.axis_index("fsdp")
    outer_count = lax.axis_size("dp") * ctx_count
    own_tokens = token_lookup(
        block_order,
        ctx_rank * local_rows + jnp.arange(local_rows, dtype=jnp.int32),
        block_size,
        local_rows,
    )
    token_stack = token_lookup(
        block_order, jnp.arange(ctx_count * local_rows, dtype=jnp.int32), block_size, local_rows
    ).reshape(ctx_count, local_rows)
    residual_in = tokens[0].astype(jnp.float32)
    grad_out = cotangent[0]
    gathered = (
        lax.all_gather(w_query, "fsdp", axis=0, tiled=True),
        lax.all_gather(key_weight, "fsdp", axis=0, tiled=True),
        lax.all_gather(value_weight, "fsdp", axis=0, tiled=True),
        lax.all_gather(w_out, "fsdp", axis=0, tiled=True),
        lax.all_gather(w_gate, "fsdp", axis=0, tiled=True),
        lax.all_gather(w_up, "fsdp", axis=0, tiled=True),
        lax.all_gather(w_down, "fsdp", axis=0, tiled=True),
        lax.all_gather(attn_gain, "fsdp", axis=0, tiled=True),
        lax.all_gather(mlp_gain, "fsdp", axis=0, tiled=True),
    )
    part_query, part_key, part_value, part_out, part_gate, part_up, part_down = (
        gathered[0],
        gathered[1],
        gathered[2],
        gathered[3],
        gathered[4],
        gathered[5],
        gathered[6],
    )
    first_gain = gathered[7].astype(jnp.float32)
    second_gain = gathered[8].astype(jnp.float32)
    positions = lax.dynamic_slice_in_dim(rope_positions, shard_rank, 1, 0)
    unit_first, root_first = normalize(residual_in)
    first_normed_input = (unit_first * first_gain).astype(jnp.bfloat16)
    normed_rows = first_normed_input[None]
    cosine_table, sine_table = rope_tables(positions)
    query_matrix = apply_rotary(
        matrix_product(normed_rows, part_query), cosine_table, sine_table, 1.0
    ).astype(jnp.bfloat16)
    rotated_keys = apply_rotary(
        matrix_product(normed_rows, part_key), cosine_table, sine_table, 1.0
    ).astype(jnp.bfloat16)
    every_value = matrix_product(normed_rows, part_value).astype(jnp.bfloat16)
    key_stack, value_stack = (
        lax.all_gather(rotated_keys[None], "ctx", axis=0, tiled=True),
        lax.all_gather(every_value[None], "ctx", axis=0, tiled=True),
    )
    attended_output, log_sums = attend_forward(
        query_matrix, key_stack, value_stack, own_tokens, token_stack
    )
    attn_term = matrix_product(attended_output[0], part_out)
    hidden_res = residual_in + attn_term
    unit_second, root_second = normalize(hidden_res)
    normed_second = (unit_second * second_gain).astype(jnp.bfloat16)
    mlp_input, cot_rows = (normed_second[None], cotangent)
    gate_pre = matrix_product(mlp_input, part_gate)
    up_pre = matrix_product(mlp_input, part_up)
    sigmoid_gate = jax.nn.sigmoid(gate_pre)
    silu_gate = gate_pre * sigmoid_gate
    activated = (silu_gate * up_pre).astype(jnp.bfloat16)
    mlp_term = matrix_product(activated[0], part_down)
    output = (hidden_res + mlp_term).astype(jnp.bfloat16)
    grad_act = back_mul(cot_rows, part_down)
    grad_gate_pre = (
        grad_act * up_pre * sigmoid_gate * (1.0 + gate_pre * (1.0 - sigmoid_gate))
    ).astype(jnp.bfloat16)
    grad_up_pre = (grad_act * silu_gate).astype(jnp.bfloat16)
    grad_gate = weight_term(mlp_input, grad_gate_pre)
    grad_up = weight_term(mlp_input, grad_up_pre)
    grad_down_t = weight_term(cot_rows, activated)
    grad_normed = back_mul(grad_gate_pre[0], part_gate) + back_mul(grad_up_pre[0], part_up)
    grad_hidden, grad_second_gain = norm_back(grad_normed, unit_second, root_second, second_gain)
    grad_hidden = grad_hidden + grad_out.astype(jnp.float32)
    grad_hidden_b = grad_hidden.astype(jnp.bfloat16)
    back_input = grad_hidden_b[None]
    grad_out_t = weight_term(back_input, attended_output)
    attended_gradient = back_mul(back_input, part_out).astype(jnp.bfloat16)
    grad_query_sum, key_pieces, value_pieces = attend_backward(
        query_matrix,
        attended_gradient,
        attended_output,
        log_sums,
        own_tokens,
        key_stack,
        value_stack,
        token_stack,
    )
    key_sum, value_sum = (
        lax.psum_scatter(
            key_pieces.astype(jnp.bfloat16), "ctx", scatter_dimension=0, tiled=True
        ).astype(jnp.float32),
        lax.psum_scatter(
            value_pieces.astype(jnp.bfloat16), "ctx", scatter_dimension=0, tiled=True
        ).astype(jnp.float32),
    )
    grad_queries = apply_rotary(grad_query_sum, cosine_table, sine_table, -1.0).astype(jnp.bfloat16)
    key_gradient_b = apply_rotary(key_sum[0], cosine_table, sine_table, -1.0).astype(jnp.bfloat16)
    value_gradient_b = value_sum[0].astype(jnp.bfloat16)
    grad_wq = weight_term(normed_rows, grad_queries)
    grad_wk = weight_term(normed_rows, key_gradient_b)
    grad_wv = weight_term(normed_rows, value_gradient_b)
    grad_normed_first = (
        back_mul(grad_queries[0], part_query)
        + back_mul(key_gradient_b[0], part_key)
        + back_mul(value_gradient_b[0], part_value)
    )
    grad_input, grad_first_gain = norm_back(grad_normed_first, unit_first, root_first, first_gain)
    grad_input = (grad_hidden + grad_input).astype(jnp.bfloat16)
    gain_first = grad_first_gain.reshape(outer_count, -1)
    gain_second = grad_second_gain.reshape(outer_count, -1)
    summed = (
        lax.psum_scatter(
            grad_wq.astype(jnp.bfloat16), "fsdp", scatter_dimension=1, tiled=True
        ).astype(jnp.float32),
        lax.psum_scatter(
            grad_wk.astype(jnp.bfloat16), "fsdp", scatter_dimension=1, tiled=True
        ).astype(jnp.float32),
        lax.psum_scatter(
            grad_wv.astype(jnp.bfloat16), "fsdp", scatter_dimension=1, tiled=True
        ).astype(jnp.float32),
        lax.psum_scatter(
            grad_out_t.astype(jnp.bfloat16), "fsdp", scatter_dimension=1, tiled=True
        ).astype(jnp.float32),
        lax.psum_scatter(
            grad_gate.astype(jnp.bfloat16), "fsdp", scatter_dimension=1, tiled=True
        ).astype(jnp.float32),
        lax.psum_scatter(
            grad_up.astype(jnp.bfloat16), "fsdp", scatter_dimension=1, tiled=True
        ).astype(jnp.float32),
        lax.psum_scatter(
            grad_down_t.astype(jnp.bfloat16), "fsdp", scatter_dimension=1, tiled=True
        ).astype(jnp.float32),
        lax.psum_scatter(
            gain_first.astype(jnp.bfloat16), "fsdp", scatter_dimension=1, tiled=True
        ).astype(jnp.float32),
        lax.psum_scatter(
            gain_second.astype(jnp.bfloat16), "fsdp", scatter_dimension=1, tiled=True
        ).astype(jnp.float32),
    )
    col_query, col_key, col_value, col_out, col_gate, col_up, col_down = (
        summed[0],
        summed[1],
        summed[2],
        summed[3],
        summed[4],
        summed[5],
        summed[6],
    )
    gain_first, gain_second = (summed[7], summed[8])
    reduced = (
        lax.psum_scatter(
            col_query.astype(jnp.bfloat16), ("dp", "ctx"), scatter_dimension=0, tiled=True
        ).astype(jnp.float32),
        lax.psum_scatter(
            col_key.astype(jnp.bfloat16), ("dp", "ctx"), scatter_dimension=0, tiled=True
        ).astype(jnp.float32),
        lax.psum_scatter(
            col_value.astype(jnp.bfloat16), ("dp", "ctx"), scatter_dimension=0, tiled=True
        ).astype(jnp.float32),
        lax.psum_scatter(
            col_out.astype(jnp.bfloat16), ("dp", "ctx"), scatter_dimension=0, tiled=True
        ).astype(jnp.float32),
        lax.psum_scatter(
            col_gate.astype(jnp.bfloat16), ("dp", "ctx"), scatter_dimension=0, tiled=True
        ).astype(jnp.float32),
        lax.psum_scatter(
            col_up.astype(jnp.bfloat16), ("dp", "ctx"), scatter_dimension=0, tiled=True
        ).astype(jnp.float32),
        lax.psum_scatter(
            col_down.astype(jnp.bfloat16), ("dp", "ctx"), scatter_dimension=0, tiled=True
        ).astype(jnp.float32),
        lax.psum_scatter(
            gain_first.astype(jnp.bfloat16), ("dp", "ctx"), scatter_dimension=0, tiled=True
        ).astype(jnp.float32),
        lax.psum_scatter(
            gain_second.astype(jnp.bfloat16), ("dp", "ctx"), scatter_dimension=0, tiled=True
        ).astype(jnp.float32),
    )
    return (
        output[None],
        grad_input[None],
        reduced[0],
        reduced[1],
        reduced[2],
        reduced[3].T,
        reduced[4],
        reduced[5],
        reduced[6].T,
        reduced[7].reshape(-1),
        reduced[8].reshape(-1),
    )


def flip(values, axis, bit):
    size = lax.axis_size(axis)
    return lax.ppermute(values, axis, [(i, i ^ bit) for i in range(size)])


def gather_plane(block):
    half = block.shape[0] // 2
    low, high = block[:half], block[half:]
    low_x = flip(low, "ctx", 1)
    high_y = flip(high, "fsdp", 2)
    low_y = flip(low, "fsdp", 2)
    high_x = flip(high, "ctx", 1)
    low_xy = flip(low_x, "fsdp", 2)
    high_xy = flip(high_y, "ctx", 1)
    near = [[(low, high), (low_x, high_x)], [(low_y, high_y), (low_xy, high_xy)]]
    far = [
        [tuple(flip(part, "fsdp", 1) for part in near[y][x]) for x in range(2)] for y in range(2)
    ]
    return [
        [jnp.concatenate(side[y][x], axis=0) for x in range(2)]
        for y in range(2)
        for side in (near, far)
    ]


def scatter_plane(partial):
    fours = partial.reshape((2, 2, 2) + partial.shape[2:])
    got = flip(fours[:, 1].astype(jnp.bfloat16), "fsdp", 1)
    both = fours[:, 0] + got.astype(jnp.float32)
    half = both.shape[2] // 2
    low, high = both[:, :, :half], both[:, :, half:]
    low_got = flip(low[1].astype(jnp.bfloat16), "fsdp", 2)
    high_got = flip(high[:, 1].astype(jnp.bfloat16), "ctx", 1)
    low = low[0] + low_got.astype(jnp.float32)
    high = high[:, 0] + high_got.astype(jnp.float32)
    low_got = flip(low[1].astype(jnp.bfloat16), "ctx", 1)
    high_got = flip(high[1].astype(jnp.bfloat16), "fsdp", 2)
    return jnp.concatenate(
        [low[0] + low_got.astype(jnp.float32), high[0] + high_got.astype(jnp.float32)], axis=0
    )


def gather_rows(own):
    shard = lax.axis_index("fsdp")
    across = flip(own, "fsdp", 2)
    parts = [own, flip(own, "fsdp", 1), across, flip(across, "fsdp", 1)]
    return parts, shard


def place(parts, shard):
    rows, width = parts[0].shape
    whole = jnp.zeros((len(parts) * rows, width), parts[0].dtype)
    for k, part in enumerate(parts):
        whole = lax.dynamic_update_slice(whole, part, ((shard ^ k) * rows, 0))
    return whole


def columns_for(weight, shard, relative, ctx_rank, ctx_count, shards):
    width = weight.shape[1] // (shards * ctx_count)
    start = ((shard ^ relative) * ctx_count + ctx_rank) * width
    return lax.dynamic_slice_in_dim(weight, start, width, 1)


def exchange_columns(weights, shard, ctx_rank, ctx_count, shards):
    parts = []
    for k in range(shards):
        piece = jnp.concatenate(
            [columns_for(w, shard, k, ctx_rank, ctx_count, shards) for w in weights], axis=1
        )
        if k:
            piece = lax.ppermute(piece, "fsdp", [(i, i ^ k) for i in range(shards)])
        parts.append(piece)
    return place(parts, shard)


def reduce_pieces(make_piece):
    sent_far = flip(
        jnp.stack([make_piece(1), make_piece(3)]).astype(jnp.bfloat16), "dp", 1
    ).astype(jnp.float32)
    far = make_piece(2) + sent_far[1]
    own = make_piece(0) + sent_far[0]
    return own + flip(far.astype(jnp.bfloat16), "dp", 2).astype(jnp.float32)


def plane_device(
    tokens,
    cotangent,
    rope_positions,
    block_order,
    w_query,
    key_weight,
    value_weight,
    w_out,
    w_gate,
    w_up,
    w_down,
    attn_gain,
    mlp_gain,
):
    f32, b16 = jnp.float32, jnp.bfloat16
    rows, width = tokens.shape[1:]
    block_size = rows // 2
    ctx_count = lax.axis_size("ctx")
    shards = lax.axis_size("fsdp")
    planes = lax.axis_size("dp")
    ctx_rank = lax.axis_index("ctx")
    shard = lax.axis_index("fsdp")
    plane = lax.axis_index("dp")
    outer_count = planes * ctx_count
    all_rows = shards * ctx_count * rows
    q_heads = QUERY_HEADS // (shards * ctx_count)
    kv_heads = KEY_VALUE_HEADS // (shards * ctx_count)
    group = q_heads // kv_heads
    score_scale = HEAD_SIZE ** (-0.5)

    x_parts = gather_plane(tokens[0])
    qkv_weight = exchange_columns(
        (w_query, key_weight, value_weight), shard, ctx_rank, ctx_count, shards
    )
    gains = jnp.stack([attn_gain, mlp_gain])
    gains = lax.all_gather(gains, "fsdp", axis=1, tiled=True).astype(f32)
    first_gain, second_gain = gains[0], gains[1]
    out_rows = w_out.shape[0] // ctx_count
    own_out = lax.dynamic_slice_in_dim(w_out, ctx_rank * out_rows, out_rows, 0)
    other_out = lax.dynamic_slice_in_dim(w_out, (1 - ctx_rank) * out_rows, out_rows, 0)
    out_parts, unused = gather_rows(jnp.concatenate([own_out, other_out], axis=0))
    glu_weight = exchange_columns((w_gate, w_up), shard, ctx_rank, ctx_count, shards)
    c_parts = gather_plane(cotangent[0])
    down_rows = w_down.shape[0] // ctx_count
    own_down = lax.dynamic_slice_in_dim(w_down, ctx_rank * down_rows, down_rows, 0)

    def joined(parts):
        return jnp.concatenate([parts[j][k] for j in range(shards) for k in range(ctx_count)], axis=0)

    pos = jnp.stack([rope_positions, flip(rope_positions, "ctx", 1)], axis=1)
    pos = jnp.stack([lax.dynamic_index_in_dim(pos, shard ^ j, 0, keepdims=False) for j in range(shards)])
    cosine_table, sine_table = rope_tables(pos.reshape(shards, ctx_count * rows))
    own_ids = jnp.arange(rows, dtype=jnp.int32)
    seq_tokens = jnp.concatenate(
        [
            token_lookup(block_order, (ctx_rank ^ k) * rows + own_ids, block_size, rows)
            for k in range(ctx_count)
        ]
    )
    allowed = seq_tokens[None, :] <= seq_tokens[:, None]

    x_all = joined(x_parts).astype(f32)
    unit_first, root_first = normalize(x_all)
    normed_first = (unit_first * first_gain).astype(b16)
    qkv = matrix_product(normed_first, qkv_weight).reshape(shards, ctx_count * rows, -1)
    q_width, kv_width = q_heads * HEAD_SIZE, kv_heads * HEAD_SIZE
    queries = apply_rotary(qkv[..., :q_width], cosine_table, sine_table, 1.0).astype(b16)
    keys = apply_rotary(
        qkv[..., q_width : q_width + kv_width], cosine_table, sine_table, 1.0
    ).astype(b16)
    values = qkv[..., q_width + kv_width :].astype(b16)
    heads_q = queries.reshape(shards, ctx_count * rows, kv_heads, group, HEAD_SIZE)
    heads_k = keys.reshape(shards, ctx_count * rows, kv_heads, HEAD_SIZE)
    heads_v = values.reshape(shards, ctx_count * rows, kv_heads, HEAD_SIZE)
    scores = (
        jnp.einsum("sqngd,sknd->sngqk", heads_q, heads_k, preferred_element_type=f32) * score_scale
    )
    scores = jnp.where(allowed, scores, masked_score)
    row_max = jnp.max(scores, axis=-1, keepdims=True)
    weights_now = jnp.where(allowed, jnp.exp(scores - row_max), 0.0)
    prob = weights_now / jnp.sum(weights_now, axis=-1, keepdims=True)
    prob_b = prob.astype(b16)
    attended = (
        jnp.einsum("sngqk,sknd->sqngd", prob_b, heads_v, preferred_element_type=f32)
        .reshape(all_rows, q_width)
        .astype(b16)
    )
    a_parts = gather_plane(attended)
    attn_term = 0.0
    for j in range(shards):
        for k in range(ctx_count):
            part = a_parts[j][k].reshape(shards, ctx_count, rows, q_width)
            ordered = jnp.concatenate(
                [part[s ^ j, t ^ k] for s in range(shards) for t in range(ctx_count)], axis=0
            )
            attn_term = attn_term + matrix_product(
                ordered, out_parts[j][k * out_rows : (k + 1) * out_rows]
            )
    hidden = x_all + attn_term
    unit_second, root_second = normalize(hidden)
    normed_second = (unit_second * second_gain).astype(b16)
    glu = matrix_product(normed_second, glu_weight)
    ff_width = glu.shape[1] // 2
    gate_pre, up_pre = glu[:, :ff_width], glu[:, ff_width:]
    sigmoid_gate = jax.nn.sigmoid(gate_pre)
    silu_gate = gate_pre * sigmoid_gate
    activated = (silu_gate * up_pre).astype(b16)
    cot_all = joined(c_parts)
    grad_act = back_mul(cot_all, own_down)
    grad_gate_pre = (
        grad_act * up_pre * sigmoid_gate * (1.0 + gate_pre * (1.0 - sigmoid_gate))
    ).astype(b16)
    grad_up_pre = (grad_act * silu_gate).astype(b16)
    grad_glu = jnp.concatenate([grad_gate_pre, grad_up_pre], axis=1)

    def four(partial):
        return partial.reshape(shards, ctx_count, rows, width)

    grad_normed = scatter_plane(four(back_mul(grad_glu, glu_weight)))
    own_unit2, own_root2 = unit_second[:rows], root_second[:rows]
    grad_hidden, grad_second_gain = norm_back(grad_normed, own_unit2, own_root2, second_gain)
    grad_hidden = grad_hidden + cotangent[0].astype(f32)
    h_parts = gather_plane(grad_hidden.astype(b16))
    grad_hidden_all = joined(h_parts)

    piece = width // planes

    def column_piece(values, j):
        return lax.dynamic_slice_in_dim(values, (plane ^ j) * piece, piece, 1)

    def product_t(left, right):
        return lax.dot_general(left, right, (((0,), (0,)), ((), ())), preferred_element_type=f32)

    glu_piece = reduce_pieces(lambda j: product_t(column_piece(normed_second, j), grad_glu))
    down_piece = reduce_pieces(lambda j: product_t(activated, column_piece(cot_all, j)))
    mlp_term = scatter_plane(four(matrix_product(activated, own_down)))
    output = (hidden[:rows] + mlp_term).astype(b16)

    grad_attended = back_mul(grad_hidden_all, own_out).astype(b16)
    head_gradient = grad_attended.reshape(shards, ctx_count * rows, kv_heads, group, HEAD_SIZE)
    head_outputs = attended.astype(f32).reshape(head_gradient.shape)
    row_delta = jnp.transpose(
        jnp.sum(head_gradient.astype(f32) * head_outputs, axis=-1), (0, 2, 3, 1)
    )
    grad_prob = jnp.einsum("sqngd,sknd->sngqk", head_gradient, heads_v, preferred_element_type=f32)
    grad_scores = (prob * (grad_prob - row_delta[..., None]) * score_scale).astype(b16)
    grad_v = jnp.einsum("sngqk,sqngd->sknd", prob_b, head_gradient, preferred_element_type=f32)
    grad_k = jnp.einsum("sngqk,sqngd->sknd", grad_scores, heads_q, preferred_element_type=f32)
    grad_q = jnp.einsum("sngqk,sknd->sqngd", grad_scores, heads_k, preferred_element_type=f32)
    seq_rows = (shards, ctx_count * rows)
    d_query = apply_rotary(grad_q.reshape(seq_rows + (-1,)), cosine_table, sine_table, -1.0)
    d_key = apply_rotary(grad_k.reshape(seq_rows + (-1,)), cosine_table, sine_table, -1.0)
    d_value = grad_v.reshape(seq_rows + (-1,))
    d_qkv = jnp.concatenate([d_query, d_key, d_value], axis=-1).astype(b16).reshape(all_rows, -1)
    grad_normed_first = scatter_plane(four(back_mul(d_qkv, qkv_weight)))
    grad_input, grad_first_gain = norm_back(
        grad_normed_first, unit_first[:rows], root_first[:rows], first_gain
    )
    grad_input = (grad_hidden + grad_input).astype(b16)
    out_piece = reduce_pieces(lambda j: product_t(attended, column_piece(grad_hidden_all, j)))
    qkv_piece = reduce_pieces(lambda j: product_t(column_piece(normed_first, j), d_qkv))
    gain_grads = lax.psum_scatter(
        jnp.stack([grad_first_gain, grad_second_gain], axis=1).reshape(outer_count * shards, -1),
        ("dp", "ctx", "fsdp"),
        scatter_dimension=0,
        tiled=True,
    ).reshape(-1, 2)

    def swap_rows(value):
        half = value.shape[0] // ctx_count
        keep = lax.dynamic_slice_in_dim(value, ctx_rank * half, half, 0)
        give = lax.dynamic_slice_in_dim(value, (1 - ctx_rank) * half, half, 0).astype(b16)
        return keep, flip(give, "ctx", 1).astype(f32)

    def wide(keep, got):
        return jnp.where(
            ctx_rank == 0,
            jnp.concatenate([keep, got], axis=1),
            jnp.concatenate([got, keep], axis=1),
        )

    def swap_columns(value):
        half = value.shape[1] // ctx_count
        keep = lax.dynamic_slice_in_dim(value, ctx_rank * half, half, 1)
        give = lax.dynamic_slice_in_dim(value, (1 - ctx_rank) * half, half, 1).astype(b16)
        got = flip(give, "ctx", 1).astype(f32)
        return jnp.where(
            ctx_rank == 0,
            jnp.concatenate([keep, got], axis=0),
            jnp.concatenate([got, keep], axis=0),
        )

    glu_keep, glu_got = swap_rows(glu_piece)
    qkv_keep, qkv_got = swap_rows(qkv_piece)
    return (
        output[None],
        grad_input[None],
        wide(qkv_keep[:, :q_width], qkv_got[:, :q_width]),
        wide(
            qkv_keep[:, q_width : q_width + kv_width], qkv_got[:, q_width : q_width + kv_width]
        ),
        wide(qkv_keep[:, q_width + kv_width :], qkv_got[:, q_width + kv_width :]),
        swap_columns(out_piece),
        wide(glu_keep[:, :ff_width], glu_got[:, :ff_width]),
        wide(glu_keep[:, ff_width:], glu_got[:, ff_width:]),
        swap_columns(down_piece),
        gain_grads[:, 0],
        gain_grads[:, 1],
    )


def plane_fits(mesh):
    sizes = mesh.shape
    return (
        sizes["ctx"] == 2
        and sizes["fsdp"] == 4
        and sizes["dp"] == 4
        and KEY_VALUE_HEADS % (sizes["ctx"] * sizes["fsdp"]) == 0
    )


def solution(mesh):
    placed = (
        P(("dp", "fsdp"), "ctx", None),
        P(("dp", "fsdp"), "ctx", None),
        P("dp", "ctx"),
        P(),
        P("fsdp", None),
        P("fsdp", None),
        P("fsdp", None),
        P("fsdp", None),
        P("fsdp", None),
        P("fsdp", None),
        P("fsdp", None),
        P("fsdp"),
        P("fsdp"),
    )
    return jax.shard_map(
        plane_device if plane_fits(mesh) else per_device,
        mesh=mesh,
        in_specs=placed,
        out_specs=(
            P(("dp", "fsdp"), "ctx", None),
            P(("dp", "fsdp"), "ctx", None),
            P(("dp", "ctx"), "fsdp"),
            P(("dp", "ctx"), "fsdp"),
            P(("dp", "ctx"), "fsdp"),
            P("fsdp", ("dp", "ctx")),
            P(("dp", "ctx"), "fsdp"),
            P(("dp", "ctx"), "fsdp"),
            P("fsdp", ("dp", "ctx")),
            P(("dp", "ctx", "fsdp")),
            P(("dp", "ctx", "fsdp")),
        ),
        check_vma=False,
    )
```

```python
import jax
import jax.numpy as jnp
from jax import lax
from jax.experimental import pallas as pl
from jax.experimental.pallas import tpu as pltpu
from jax.sharding import PartitionSpec as P

QUERY_HEADS = 16
KEY_VALUE_HEADS = 8
HEAD_SIZE = 96


rope_base = 100000.0
norm_eps = 1e-05
masked_score = -1e30


def matrix_product(left, right):
    return jnp.dot(left, right, preferred_element_type=jnp.float32)


def back_mul(left, right):
    return lax.dot_general(
        left, right, (((left.ndim - 1,), (1,)), ((), ())), preferred_element_type=jnp.float32
    )


def weight_term(left, right):
    return lax.dot_general(
        left, right, (((0, 1), (0, 1)), ((), ())), preferred_element_type=jnp.float32
    )


def rope_tables(positions):
    half_dim = HEAD_SIZE // 2
    inverse = rope_base ** (-2.0 * jnp.arange(half_dim, dtype=jnp.float32) / HEAD_SIZE)
    angles = positions.astype(jnp.float32)[..., None] * inverse
    return (jnp.cos(angles), jnp.sin(angles))


def apply_rotary(values, cosine_table, sine_table, direction):
    leading = values.shape[:-1]
    head_count = values.shape[-1] // HEAD_SIZE
    half_dim = HEAD_SIZE // 2
    halves = values.reshape(leading + (head_count, 2, half_dim))
    first_half = halves[..., 0, :]
    second_half = halves[..., 1, :]
    cos_part = cosine_table[..., None, :]
    sin_part = direction * sine_table[..., None, :]
    joined = jnp.stack(
        [
            first_half * cos_part - second_half * sin_part,
            second_half * cos_part + first_half * sin_part,
        ],
        axis=-2,
    )
    return joined.reshape(leading + (head_count * HEAD_SIZE,))


def normalize(values):
    inv_root = lax.rsqrt(jnp.mean(values * values, axis=-1, keepdims=True) + norm_eps)
    return (values * inv_root, inv_root)


def norm_back(grad_output, unit_rows, inv_root, gain_vec):
    grad_unit = grad_output * gain_vec
    grad_gain = jnp.sum(grad_output * unit_rows, axis=0)
    grad_input = inv_root * (
        grad_unit - unit_rows * jnp.mean(grad_unit * unit_rows, axis=-1, keepdims=True)
    )
    return (grad_input, grad_gain)


def token_lookup(block_order, row_ids, block_size, local_rows):
    slot_ids = 2 * (row_ids // local_rows) + row_ids % local_rows // block_size
    onehot_table = (
        slot_ids[:, None] == jnp.arange(block_order.shape[0], dtype=jnp.int32)[None, :]
    ).astype(jnp.int32)
    chosen = jnp.sum(onehot_table * block_order[None, :], axis=1)
    return chosen * block_size + row_ids % block_size


def attend_forward(query_matrix, key_stack, value_stack, own_tokens, token_stack):
    seq_count = query_matrix.shape[0]
    count_of_rows = query_matrix.shape[1]
    kv_heads = key_stack.shape[-1] // HEAD_SIZE
    query_group_width = QUERY_HEADS // KEY_VALUE_HEADS
    score_scale = HEAD_SIZE ** (-0.5)
    head_queries = query_matrix.reshape(
        seq_count, count_of_rows, kv_heads, query_group_width, HEAD_SIZE
    )

    def absorb(state, block_in):
        running_max, running_sum, weighted = state
        piece_keys, piece_values, piece_tokens = block_in
        piece_rows = piece_keys.shape[1]
        scores = (
            jnp.einsum(
                "sqngd,sknd->sngqk",
                head_queries,
                piece_keys.reshape(seq_count, piece_rows, kv_heads, HEAD_SIZE),
                preferred_element_type=jnp.float32,
            )
            * score_scale
        )
        allowed = piece_tokens[None, None, None, None, :] <= own_tokens[None, None, None, :, None]
        scores = jnp.where(allowed, scores, masked_score)
        new_max = jnp.maximum(running_max, jnp.max(scores, axis=-1))
        weights_now = jnp.where(allowed, jnp.exp(scores - new_max[..., None]), 0.0)
        decay_factor = jnp.exp(running_max - new_max)
        new_sum = running_sum * decay_factor + jnp.sum(weights_now, axis=-1)
        block_sum = jnp.einsum(
            "sngqk,sknd->sngqd",
            weights_now.astype(jnp.bfloat16),
            piece_values.reshape(seq_count, piece_rows, kv_heads, HEAD_SIZE),
            preferred_element_type=jnp.float32,
        )
        return ((new_max, new_sum, weighted * decay_factor[..., None] + block_sum), 0)

    stat_shape = (seq_count, kv_heads, query_group_width, count_of_rows)
    start_state = (
        jnp.full(stat_shape, masked_score, jnp.float32),
        jnp.zeros(stat_shape, jnp.float32),
        jnp.zeros(stat_shape + (HEAD_SIZE,), jnp.float32),
    )
    (running_max, running_sum, weighted), unused = lax.scan(
        absorb, start_state, (key_stack, value_stack, token_stack)
    )
    attended_output = (
        jnp.transpose(weighted / running_sum[..., None], (0, 3, 1, 2, 4))
        .reshape(seq_count, count_of_rows, kv_heads * query_group_width * HEAD_SIZE)
        .astype(jnp.bfloat16)
    )
    return (attended_output, running_max + jnp.log(running_sum))


def attend_backward(
    query_matrix,
    attended_gradient,
    attended_output,
    log_sums,
    own_tokens,
    key_stack,
    value_stack,
    token_stack,
):
    seq_count = query_matrix.shape[0]
    count_of_rows = query_matrix.shape[1]
    kv_heads = key_stack.shape[-1] // HEAD_SIZE
    query_group_width = QUERY_HEADS // KEY_VALUE_HEADS
    score_scale = HEAD_SIZE ** (-0.5)
    head_queries = query_matrix.reshape(
        seq_count, count_of_rows, kv_heads, query_group_width, HEAD_SIZE
    )
    head_gradient = attended_gradient.reshape(
        seq_count, count_of_rows, kv_heads, query_group_width, HEAD_SIZE
    )
    head_outputs = attended_output.astype(jnp.float32).reshape(
        seq_count, count_of_rows, kv_heads, query_group_width, HEAD_SIZE
    )
    row_delta = jnp.transpose(
        jnp.sum(head_gradient.astype(jnp.float32) * head_outputs, axis=-1), (0, 2, 3, 1)
    )

    def key_step(grad_query_sum, block_in):
        piece_keys, piece_values, piece_tokens = block_in
        piece_rows = piece_keys.shape[1]
        head_keys = piece_keys.reshape(seq_count, piece_rows, kv_heads, HEAD_SIZE)
        head_values = piece_values.reshape(seq_count, piece_rows, kv_heads, HEAD_SIZE)
        scores = (
            jnp.einsum(
                "sqngd,sknd->sngqk", head_queries, head_keys, preferred_element_type=jnp.float32
            )
            * score_scale
        )
        allowed = piece_tokens[None, None, None, None, :] <= own_tokens[None, None, None, :, None]
        scores = jnp.where(allowed, scores, masked_score)
        attn_prob = jnp.where(allowed, jnp.exp(scores - log_sums[..., None]), 0.0)
        grad_prob = jnp.einsum(
            "sqngd,sknd->sngqk", head_gradient, head_values, preferred_element_type=jnp.float32
        )
        grad_scores = (attn_prob * (grad_prob - row_delta[..., None]) * score_scale).astype(
            jnp.bfloat16
        )
        grad_value_piece = jnp.einsum(
            "sngqk,sqngd->sknd",
            attn_prob.astype(jnp.bfloat16),
            head_gradient,
            preferred_element_type=jnp.float32,
        )
        grad_key_piece = jnp.einsum(
            "sngqk,sqngd->sknd", grad_scores, head_queries, preferred_element_type=jnp.float32
        )
        grad_query_sum = grad_query_sum + jnp.einsum(
            "sngqk,sknd->sqngd", grad_scores, head_keys, preferred_element_type=jnp.float32
        )
        return (
            grad_query_sum,
            (
                grad_key_piece.reshape(seq_count, piece_rows, kv_heads * HEAD_SIZE),
                grad_value_piece.reshape(seq_count, piece_rows, kv_heads * HEAD_SIZE),
            ),
        )

    zero_query = jnp.zeros(
        (seq_count, count_of_rows, kv_heads, query_group_width, HEAD_SIZE), jnp.float32
    )
    grad_query_sum, (key_pieces, value_pieces) = lax.scan(
        key_step, zero_query, (key_stack, value_stack, token_stack)
    )
    return (
        grad_query_sum.reshape(seq_count, count_of_rows, kv_heads * query_group_width * HEAD_SIZE),
        key_pieces,
        value_pieces,
    )


def per_device(
    tokens,
    cotangent,
    rope_positions,
    block_order,
    w_query,
    key_weight,
    value_weight,
    w_out,
    w_gate,
    w_up,
    w_down,
    attn_gain,
    mlp_gain,
):
    local_rows = tokens.shape[1]
    block_size = local_rows // 2
    ctx_count = lax.axis_size("ctx")
    ctx_rank = lax.axis_index("ctx")
    shard_rank = lax.axis_index("fsdp")
    outer_count = lax.axis_size("dp") * ctx_count
    own_tokens = token_lookup(
        block_order,
        ctx_rank * local_rows + jnp.arange(local_rows, dtype=jnp.int32),
        block_size,
        local_rows,
    )
    token_stack = token_lookup(
        block_order, jnp.arange(ctx_count * local_rows, dtype=jnp.int32), block_size, local_rows
    ).reshape(ctx_count, local_rows)
    residual_in = tokens[0].astype(jnp.float32)
    grad_out = cotangent[0]
    gathered = (
        lax.all_gather(w_query, "fsdp", axis=0, tiled=True),
        lax.all_gather(key_weight, "fsdp", axis=0, tiled=True),
        lax.all_gather(value_weight, "fsdp", axis=0, tiled=True),
        lax.all_gather(w_out, "fsdp", axis=0, tiled=True),
        lax.all_gather(w_gate, "fsdp", axis=0, tiled=True),
        lax.all_gather(w_up, "fsdp", axis=0, tiled=True),
        lax.all_gather(w_down, "fsdp", axis=0, tiled=True),
        lax.all_gather(attn_gain, "fsdp", axis=0, tiled=True),
        lax.all_gather(mlp_gain, "fsdp", axis=0, tiled=True),
    )
    part_query, part_key, part_value, part_out, part_gate, part_up, part_down = (
        gathered[0],
        gathered[1],
        gathered[2],
        gathered[3],
        gathered[4],
        gathered[5],
        gathered[6],
    )
    first_gain = gathered[7].astype(jnp.float32)
    second_gain = gathered[8].astype(jnp.float32)
    positions = lax.dynamic_slice_in_dim(rope_positions, shard_rank, 1, 0)
    unit_first, root_first = normalize(residual_in)
    first_normed_input = (unit_first * first_gain).astype(jnp.bfloat16)
    normed_rows = first_normed_input[None]
    cosine_table, sine_table = rope_tables(positions)
    query_matrix = apply_rotary(
        matrix_product(normed_rows, part_query), cosine_table, sine_table, 1.0
    ).astype(jnp.bfloat16)
    rotated_keys = apply_rotary(
        matrix_product(normed_rows, part_key), cosine_table, sine_table, 1.0
    ).astype(jnp.bfloat16)
    every_value = matrix_product(normed_rows, part_value).astype(jnp.bfloat16)
    key_stack, value_stack = (
        lax.all_gather(rotated_keys[None], "ctx", axis=0, tiled=True),
        lax.all_gather(every_value[None], "ctx", axis=0, tiled=True),
    )
    attended_output, log_sums = attend_forward(
        query_matrix, key_stack, value_stack, own_tokens, token_stack
    )
    attn_term = matrix_product(attended_output[0], part_out)
    hidden_res = residual_in + attn_term
    unit_second, root_second = normalize(hidden_res)
    normed_second = (unit_second * second_gain).astype(jnp.bfloat16)
    mlp_input, cot_rows = (normed_second[None], cotangent)
    gate_pre = matrix_product(mlp_input, part_gate)
    up_pre = matrix_product(mlp_input, part_up)
    sigmoid_gate = jax.nn.sigmoid(gate_pre)
    silu_gate = gate_pre * sigmoid_gate
    activated = (silu_gate * up_pre).astype(jnp.bfloat16)
    mlp_term = matrix_product(activated[0], part_down)
    output = (hidden_res + mlp_term).astype(jnp.bfloat16)
    grad_act = back_mul(cot_rows, part_down)
    grad_gate_pre = (
        grad_act * up_pre * sigmoid_gate * (1.0 + gate_pre * (1.0 - sigmoid_gate))
    ).astype(jnp.bfloat16)
    grad_up_pre = (grad_act * silu_gate).astype(jnp.bfloat16)
    grad_gate = weight_term(mlp_input, grad_gate_pre)
    grad_up = weight_term(mlp_input, grad_up_pre)
    grad_down_t = weight_term(cot_rows, activated)
    grad_normed = back_mul(grad_gate_pre[0], part_gate) + back_mul(grad_up_pre[0], part_up)
    grad_hidden, grad_second_gain = norm_back(grad_normed, unit_second, root_second, second_gain)
    grad_hidden = grad_hidden + grad_out.astype(jnp.float32)
    grad_hidden_b = grad_hidden.astype(jnp.bfloat16)
    back_input = grad_hidden_b[None]
    grad_out_t = weight_term(back_input, attended_output)
    attended_gradient = back_mul(back_input, part_out).astype(jnp.bfloat16)
    grad_query_sum, key_pieces, value_pieces = attend_backward(
        query_matrix,
        attended_gradient,
        attended_output,
        log_sums,
        own_tokens,
        key_stack,
        value_stack,
        token_stack,
    )
    key_sum, value_sum = (
        lax.psum_scatter(
            key_pieces.astype(jnp.bfloat16), "ctx", scatter_dimension=0, tiled=True
        ).astype(jnp.float32),
        lax.psum_scatter(
            value_pieces.astype(jnp.bfloat16), "ctx", scatter_dimension=0, tiled=True
        ).astype(jnp.float32),
    )
    grad_queries = apply_rotary(grad_query_sum, cosine_table, sine_table, -1.0).astype(jnp.bfloat16)
    key_gradient_b = apply_rotary(key_sum[0], cosine_table, sine_table, -1.0).astype(jnp.bfloat16)
    value_gradient_b = value_sum[0].astype(jnp.bfloat16)
    grad_wq = weight_term(normed_rows, grad_queries)
    grad_wk = weight_term(normed_rows, key_gradient_b)
    grad_wv = weight_term(normed_rows, value_gradient_b)
    grad_normed_first = (
        back_mul(grad_queries[0], part_query)
        + back_mul(key_gradient_b[0], part_key)
        + back_mul(value_gradient_b[0], part_value)
    )
    grad_input, grad_first_gain = norm_back(grad_normed_first, unit_first, root_first, first_gain)
    grad_input = (grad_hidden + grad_input).astype(jnp.bfloat16)
    gain_first = grad_first_gain.reshape(outer_count, -1)
    gain_second = grad_second_gain.reshape(outer_count, -1)
    summed = (
        lax.psum_scatter(
            grad_wq.astype(jnp.bfloat16), "fsdp", scatter_dimension=1, tiled=True
        ).astype(jnp.float32),
        lax.psum_scatter(
            grad_wk.astype(jnp.bfloat16), "fsdp", scatter_dimension=1, tiled=True
        ).astype(jnp.float32),
        lax.psum_scatter(
            grad_wv.astype(jnp.bfloat16), "fsdp", scatter_dimension=1, tiled=True
        ).astype(jnp.float32),
        lax.psum_scatter(
            grad_out_t.astype(jnp.bfloat16), "fsdp", scatter_dimension=1, tiled=True
        ).astype(jnp.float32),
        lax.psum_scatter(
            grad_gate.astype(jnp.bfloat16), "fsdp", scatter_dimension=1, tiled=True
        ).astype(jnp.float32),
        lax.psum_scatter(
            grad_up.astype(jnp.bfloat16), "fsdp", scatter_dimension=1, tiled=True
        ).astype(jnp.float32),
        lax.psum_scatter(
            grad_down_t.astype(jnp.bfloat16), "fsdp", scatter_dimension=1, tiled=True
        ).astype(jnp.float32),
        lax.psum_scatter(
            gain_first.astype(jnp.bfloat16), "fsdp", scatter_dimension=1, tiled=True
        ).astype(jnp.float32),
        lax.psum_scatter(
            gain_second.astype(jnp.bfloat16), "fsdp", scatter_dimension=1, tiled=True
        ).astype(jnp.float32),
    )
    col_query, col_key, col_value, col_out, col_gate, col_up, col_down = (
        summed[0],
        summed[1],
        summed[2],
        summed[3],
        summed[4],
        summed[5],
        summed[6],
    )
    gain_first, gain_second = (summed[7], summed[8])
    reduced = (
        lax.psum_scatter(
            col_query.astype(jnp.bfloat16), ("dp", "ctx"), scatter_dimension=0, tiled=True
        ).astype(jnp.float32),
        lax.psum_scatter(
            col_key.astype(jnp.bfloat16), ("dp", "ctx"), scatter_dimension=0, tiled=True
        ).astype(jnp.float32),
        lax.psum_scatter(
            col_value.astype(jnp.bfloat16), ("dp", "ctx"), scatter_dimension=0, tiled=True
        ).astype(jnp.float32),
        lax.psum_scatter(
            col_out.astype(jnp.bfloat16), ("dp", "ctx"), scatter_dimension=0, tiled=True
        ).astype(jnp.float32),
        lax.psum_scatter(
            col_gate.astype(jnp.bfloat16), ("dp", "ctx"), scatter_dimension=0, tiled=True
        ).astype(jnp.float32),
        lax.psum_scatter(
            col_up.astype(jnp.bfloat16), ("dp", "ctx"), scatter_dimension=0, tiled=True
        ).astype(jnp.float32),
        lax.psum_scatter(
            col_down.astype(jnp.bfloat16), ("dp", "ctx"), scatter_dimension=0, tiled=True
        ).astype(jnp.float32),
        lax.psum_scatter(
            gain_first.astype(jnp.bfloat16), ("dp", "ctx"), scatter_dimension=0, tiled=True
        ).astype(jnp.float32),
        lax.psum_scatter(
            gain_second.astype(jnp.bfloat16), ("dp", "ctx"), scatter_dimension=0, tiled=True
        ).astype(jnp.float32),
    )
    return (
        output[None],
        grad_input[None],
        reduced[0],
        reduced[1],
        reduced[2],
        reduced[3].T,
        reduced[4],
        reduced[5],
        reduced[6].T,
        reduced[7].reshape(-1),
        reduced[8].reshape(-1),
    )


def flip(values, axis, bit):
    size = lax.axis_size(axis)
    return lax.ppermute(values, axis, [(i, i ^ bit) for i in range(size)])


def gather_plane(low, high):
    low_x = flip(low, "ctx", 1)
    high_y = flip(high, "fsdp", 2)
    own_core = flip(jnp.stack([low, high]), "fsdp", 1)
    low_y = flip(low, "fsdp", 2)
    high_x = flip(high, "ctx", 1)
    low_xy = flip(low_x, "fsdp", 2)
    high_xy = flip(high_y, "ctx", 1)
    near_core = flip(jnp.stack([low_x, high_y, low_y, high_x]), "fsdp", 1)
    far_core = flip(jnp.stack([low_xy, high_xy]), "fsdp", 1)
    alone = [v[None] for v in (low, high, low_x, high_x, low_y, high_y, low_xy, high_xy)]
    arrays = alone + [own_core, near_core, far_core]
    source = {}
    for half in range(2):
        for dx, dy, at in ((0, 0, 0), (1, 0, 2), (0, 1, 4), (1, 1, 6)):
            source[dx, dy, 0, half] = (at + half, 0)
        source[0, 0, 1, half] = (8, half)
        source[1, 0, 1, half] = (9, 0 if half == 0 else 3)
        source[0, 1, 1, half] = (9, 2 if half == 0 else 1)
        source[1, 1, 1, half] = (10, half)
    return arrays, source


def scatter_plane(keep, send):
    f32, b16 = jnp.float32, jnp.bfloat16
    both = keep.astype(f32) + flip(send, "fsdp", 1).astype(f32)
    half = both.shape[2] // 2
    low, high = both[:, :, :half], both[:, :, half:]
    low_got = flip(low[1].astype(b16), "fsdp", 2)
    high_got = flip(high[:, 1].astype(b16), "ctx", 1)
    low = low[0] + low_got.astype(f32)
    high = high[:, 0] + high_got.astype(f32)
    low_got = flip(low[1].astype(b16), "ctx", 1)
    high_got = flip(high[1].astype(b16), "fsdp", 2)
    return jnp.concatenate(
        [low[0] + low_got.astype(f32), high[0] + high_got.astype(f32)], axis=0
    )


def gather_rows(own):
    across = flip(own, "fsdp", 2)
    return [own, flip(own, "fsdp", 1), across, flip(across, "fsdp", 1)]


def kernel_params():
    return pltpu.CompilerParams(
        vmem_limit_bytes=56 * 1024 * 1024, dimension_semantics=("arbitrary",)
    )


def whole(shape):
    return pl.BlockSpec(shape, lambda s: (0,) * len(shape))


def place(parts, shard):
    rows, width = parts[0].shape
    count = len(parts)

    def body(shard_ref, *refs):
        ins, out, sems = refs[:count], refs[count], refs[count + 1]
        copies = []
        for k in range(count):
            start = pl.multiple_of((shard_ref[0] ^ k) * rows, rows)
            copies.append(
                pltpu.make_async_copy(ins[k], out.at[pl.ds(start, rows)], sems.at[k])
            )
        for copy in copies:
            copy.start()
        for copy in copies:
            copy.wait()

    return pl.pallas_call(
        body,
        out_shape=jax.ShapeDtypeStruct((count * rows, width), parts[0].dtype),
        in_specs=[pl.BlockSpec(memory_space=pltpu.SMEM)]
        + [pl.BlockSpec(memory_space=pl.ANY)] * count,
        out_specs=pl.BlockSpec(memory_space=pl.ANY),
        scratch_shapes=[pltpu.SemaphoreType.DMA((count,))],
        name="place_rows",
    )(shard.reshape(1), *parts)


def plane_copies(refs, source, scratch, sems, core_count, ctx_count):
    copies = []
    count = 0
    for j in range(scratch.shape[0]):
        group = []
        for k in range(ctx_count):
            for half in range(2):
                at, lead = source[k, j // core_count, j % core_count, half]
                rows = refs[at].shape[1]
                start = (k * 2 + half) * rows
                group.append(
                    pltpu.make_async_copy(
                        refs[at].at[lead], scratch.at[j, pl.ds(start, rows)], sems.at[count]
                    )
                )
                count += 1
        copies.append(group)
    return copies


def arrive(copies, step):
    @pl.when(step == 0)
    def _():
        for group in copies:
            for copy in group:
                copy.start()

    for j, group in enumerate(copies):

        @pl.when(step == j)
        def _():
            for copy in group:
                copy.wait()


def swap_halves(value):
    half = HEAD_SIZE // 2
    lane = lax.broadcasted_iota(jnp.int32, value.shape, 1)
    lanes = value.shape[1]
    return jnp.where(
        lane < half, pltpu.roll(value, lanes - half, 1), pltpu.roll(value, half, 1)
    )


def nt_dot(left, right):
    return lax.dot_general(
        left, right, (((1,), (1,)), ((), ())), preferred_element_type=jnp.float32
    )


def tn_dot(left, right):
    return lax.dot_general(
        left, right, (((0,), (0,)), ((), ())), preferred_element_type=jnp.float32
    )


def head_probs(query, key, allowed):
    scores = nt_dot(query, key) * (HEAD_SIZE ** (-0.5))
    scores = jnp.where(allowed, scores, masked_score)
    row_max = jnp.max(scores, axis=-1, keepdims=True)
    weights_now = jnp.where(allowed, jnp.exp(scores - row_max), 0.0)
    return weights_now / jnp.sum(weights_now, axis=-1, keepdims=True)


def attention_forward(pieces, source, gain, weight, cosine, sine, ids_row, ids_column, shape):
    seqs, ctx_count, rows, width, heads = shape
    f32, b16 = jnp.float32, jnp.bfloat16
    seq_rows = ctx_count * rows
    lanes = weight.shape[1] // (heads + 2)
    packed = heads * HEAD_SIZE
    count = len(pieces)

    def body(*refs):
        piece_refs = refs[:count]
        gain_ref, w_ref, cos_ref, sin_ref, row_ref, col_ref = refs[count : count + 6]
        all_ref, normed_ref, qkv_ref, low_ref, high_ref, x_ref, sems = refs[count + 6 :]
        step = pl.program_id(0)
        arrive(plane_copies(piece_refs, source, x_ref, sems, 2, ctx_count), step)
        raw = x_ref[step]
        all_ref[...] = raw
        value = raw.astype(f32)
        root = lax.rsqrt(jnp.mean(value * value, axis=-1, keepdims=True) + norm_eps)
        normed = (value * root * gain_ref[...]).astype(b16)
        normed_ref[...] = normed
        qkv = jnp.dot(normed, w_ref[...], preferred_element_type=f32)
        cos, sin = cos_ref[...], sin_ref[...]
        allowed = row_ref[...] <= col_ref[...]
        parts = []
        for i in range(heads + 1):
            part = qkv[:, i * lanes : (i + 1) * lanes]
            parts.append((part * cos + swap_halves(part) * sin).astype(b16))
        parts.append(qkv[:, (heads + 1) * lanes :].astype(b16))
        for i, part in enumerate(parts):
            qkv_ref[:, i * lanes : (i + 1) * lanes] = part
        mixed = []
        for h in range(heads):
            prob = head_probs(parts[h], parts[heads], allowed).astype(b16)
            mixed.append(jnp.dot(prob, parts[heads + 1], preferred_element_type=f32))
        merged = jnp.concatenate([m[:, :HEAD_SIZE] for m in mixed], axis=1).astype(b16)
        low_ref[0] = merged[:rows]
        high_ref[0] = merged[rows:]

    block = lambda n: pl.BlockSpec((seq_rows, n), lambda s: (s, 0))
    half = pl.BlockSpec((1, rows, packed), lambda s: (s, 0, 0))
    total = seqs * seq_rows
    return pl.pallas_call(
        body,
        grid=(seqs,),
        in_specs=[pl.BlockSpec(memory_space=pl.ANY)] * count
        + [whole((1, width)), whole(weight.shape), block(lanes), block(lanes)]
        + [whole((1, seq_rows)), whole((seq_rows, 1))],
        out_specs=[block(width), block(width), block(weight.shape[1]), half, half],
        out_shape=[
            jax.ShapeDtypeStruct((total, width), b16),
            jax.ShapeDtypeStruct((total, width), b16),
            jax.ShapeDtypeStruct((total, weight.shape[1]), b16),
            jax.ShapeDtypeStruct((seqs, rows, packed), b16),
            jax.ShapeDtypeStruct((seqs, rows, packed), b16),
        ],
        scratch_shapes=[
            pltpu.VMEM((seqs, seq_rows, width), b16),
            pltpu.SemaphoreType.DMA((seqs * ctx_count * 2,)),
        ],
        compiler_params=kernel_params(),
        name="attention_forward",
    )(*pieces, gain, weight, cosine, sine, ids_row, ids_column)


def feed_forward(x_all, pieces, source, out_parts, gain, glu_weight, down, cot_all, shape):
    seqs, ctx_count, rows, width, packed = shape
    f32, b16 = jnp.float32, jnp.bfloat16
    seq_rows = ctx_count * rows
    ff = down.shape[0]
    piece_args, piece_specs = [], []
    for j in range(seqs):
        for k in range(ctx_count):
            for t in range(ctx_count):
                at, lead = source[k, j // 2, j % 2, t ^ k]
                piece_args.append(pieces[at])
                piece_specs.append(
                    pl.BlockSpec(
                        (1, 1, rows, packed), lambda s, j=j, lead=lead: (lead, s ^ j, 0, 0)
                    )
                )
    count = len(piece_args)

    def body(x_ref, *refs):
        piece_refs = refs[:count]
        out_refs = refs[count : count + seqs]
        gain_ref, glu_ref, down_ref, cot_ref = refs[count + seqs : count + seqs + 4]
        (own_ref, normed_ref, grad_ref, act_ref, gain_out, keep_ref, send_ref, mkeep_ref,
         msend_ref) = refs[count + seqs + 4 :]
        step = pl.program_id(0)
        hidden = x_ref[...].astype(f32)
        for j in range(seqs):
            for k in range(ctx_count):
                base = (j * ctx_count + k) * ctx_count
                left = jnp.concatenate(
                    [piece_refs[base + t][0, 0] for t in range(ctx_count)], axis=0
                )
                hidden = hidden + jnp.dot(
                    left, out_refs[j][k * packed : (k + 1) * packed], preferred_element_type=f32
                )

        @pl.when(step == 0)
        def _():
            own_ref[...] = hidden[:rows]
            gain_out[...] = jnp.zeros(gain_out.shape, f32)

        root = lax.rsqrt(jnp.mean(hidden * hidden, axis=-1, keepdims=True) + norm_eps)
        unit = hidden * root
        normed = (unit * gain_ref[...]).astype(b16)
        normed_ref[...] = normed
        gate = jnp.dot(normed, glu_ref[:, :ff], preferred_element_type=f32)
        up = jnp.dot(normed, glu_ref[:, ff:], preferred_element_type=f32)
        grad_act = nt_dot(cot_ref[...], down_ref[...])
        sig = jax.nn.sigmoid(gate)
        silu = gate * sig
        act = (silu * up).astype(b16)
        act_ref[...] = act
        grad_gate = (grad_act * up * sig * (1.0 + gate * (1.0 - sig))).astype(b16)
        grad_up = (grad_act * silu).astype(b16)
        grad_ref[:, :ff] = grad_gate
        grad_ref[:, ff:] = grad_up
        back = nt_dot(grad_gate, glu_ref[:, :ff]) + nt_dot(grad_up, glu_ref[:, ff:])
        gain_out[...] += jnp.sum(back * unit, axis=0, keepdims=True)
        mixed = jnp.dot(act, down_ref[...], preferred_element_type=f32)
        back = back.astype(b16).reshape(1, ctx_count, rows, width)
        mixed = mixed.astype(b16).reshape(1, ctx_count, rows, width)

        @pl.when(step % 2 == 0)
        def _():
            keep_ref[...] = back
            mkeep_ref[...] = mixed

        @pl.when(step % 2 == 1)
        def _():
            send_ref[...] = back
            msend_ref[...] = mixed

    block = lambda n: pl.BlockSpec((seq_rows, n), lambda s: (s, 0))
    paired = pl.BlockSpec((1, ctx_count, rows, width), lambda s: (s // 2, 0, 0, 0))
    total = seqs * seq_rows
    pair_shape = jax.ShapeDtypeStruct((seqs // 2, ctx_count, rows, width), b16)
    return pl.pallas_call(
        body,
        grid=(seqs,),
        in_specs=[block(width)]
        + piece_specs
        + [whole(part.shape) for part in out_parts]
        + [whole((1, width)), whole(glu_weight.shape), whole(down.shape), block(width)],
        out_specs=[whole((rows, width)), block(width), block(2 * ff), block(ff), whole((1, width))]
        + [paired] * 4,
        out_shape=[
            jax.ShapeDtypeStruct((rows, width), f32),
            jax.ShapeDtypeStruct((total, width), b16),
            jax.ShapeDtypeStruct((total, 2 * ff), b16),
            jax.ShapeDtypeStruct((total, ff), b16),
            jax.ShapeDtypeStruct((1, width), f32),
        ]
        + [pair_shape] * 4,
        compiler_params=kernel_params(),
        name="feed_forward",
    )(x_all, *piece_args, *out_parts, gain, glu_weight, down, cot_all)


def attention_backward(
    pieces, source, out_weight, weight, qkv, x_all, cosine, sine, ids_row, ids_column, shape
):
    seqs, ctx_count, rows, width, heads = shape
    f32, b16 = jnp.float32, jnp.bfloat16
    seq_rows = ctx_count * rows
    lanes = weight.shape[1] // (heads + 2)
    packed = heads * HEAD_SIZE
    count = len(pieces)
    score_scale = HEAD_SIZE ** (-0.5)

    def body(*refs):
        piece_refs = refs[:count]
        out_ref, w_ref, qkv_ref, xin_ref, cos_ref, sin_ref, row_ref, col_ref = refs[
            count : count + 8
        ]
        all_ref, att_ref, d_ref, gain_out, keep_ref, send_ref, h_ref, sems = refs[count + 8 :]
        step = pl.program_id(0)
        arrive(plane_copies(piece_refs, source, h_ref, sems, 2, ctx_count), step)
        grad_hidden = h_ref[step]
        all_ref[...] = grad_hidden
        grad_attended = nt_dot(grad_hidden, out_ref[...]).astype(b16)
        cos, sin = cos_ref[...], sin_ref[...]
        allowed = row_ref[...] <= col_ref[...]
        key = qkv_ref[:, heads * lanes : (heads + 1) * lanes]
        value = qkv_ref[:, (heads + 1) * lanes :]
        grad_key, grad_value, mixed = 0.0, 0.0, []
        for h in range(heads):
            query = qkv_ref[:, h * lanes : (h + 1) * lanes]
            grad_head = grad_attended[:, h * lanes : (h + 1) * lanes]
            prob = head_probs(query, key, allowed)
            prob_b = prob.astype(b16)
            head_out = jnp.dot(prob_b, value, preferred_element_type=f32).astype(b16)
            mixed.append(head_out[:, :HEAD_SIZE].astype(f32))
            delta = jnp.sum(
                grad_head.astype(f32) * head_out.astype(f32), axis=-1, keepdims=True
            )
            grad_prob = nt_dot(grad_head, value)
            grad_scores = (prob * (grad_prob - delta) * score_scale).astype(b16)
            grad_query = jnp.dot(grad_scores, key, preferred_element_type=f32)
            d_ref[:, h * lanes : (h + 1) * lanes] = (
                grad_query * cos - swap_halves(grad_query) * sin
            ).astype(b16)
            grad_key = grad_key + tn_dot(grad_scores, query)
            grad_value = grad_value + tn_dot(prob_b, grad_head)
        att_ref[...] = jnp.concatenate(mixed, axis=1).astype(b16)
        d_ref[:, heads * lanes : (heads + 1) * lanes] = (
            grad_key * cos - swap_halves(grad_key) * sin
        ).astype(b16)
        d_ref[:, (heads + 1) * lanes :] = grad_value.astype(b16)
        back = nt_dot(d_ref[...], w_ref[...])
        x = xin_ref[...].astype(f32)
        unit = x * lax.rsqrt(jnp.mean(x * x, axis=-1, keepdims=True) + norm_eps)

        @pl.when(step == 0)
        def _():
            gain_out[...] = jnp.zeros(gain_out.shape, f32)

        gain_out[...] += jnp.sum(back * unit, axis=0, keepdims=True)
        back = back.astype(b16).reshape(1, ctx_count, rows, width)

        @pl.when(step % 2 == 0)
        def _():
            keep_ref[...] = back

        @pl.when(step % 2 == 1)
        def _():
            send_ref[...] = back

    block = lambda n: pl.BlockSpec((seq_rows, n), lambda s: (s, 0))
    paired = pl.BlockSpec((1, ctx_count, rows, width), lambda s: (s // 2, 0, 0, 0))
    total = seqs * seq_rows
    pair_shape = jax.ShapeDtypeStruct((seqs // 2, ctx_count, rows, width), b16)
    return pl.pallas_call(
        body,
        grid=(seqs,),
        in_specs=[pl.BlockSpec(memory_space=pl.ANY)] * count
        + [whole(out_weight.shape), whole(weight.shape), block(weight.shape[1]), block(width)]
        + [block(lanes), block(lanes), whole((1, seq_rows)), whole((seq_rows, 1))],
        out_specs=[block(width), block(packed), block(weight.shape[1]), whole((1, width))]
        + [paired] * 2,
        out_shape=[
            jax.ShapeDtypeStruct((total, width), b16),
            jax.ShapeDtypeStruct((total, packed), b16),
            jax.ShapeDtypeStruct((total, weight.shape[1]), b16),
            jax.ShapeDtypeStruct((1, width), f32),
        ]
        + [pair_shape] * 2,
        scratch_shapes=[
            pltpu.VMEM((seqs, seq_rows, width), b16),
            pltpu.SemaphoreType.DMA((seqs * ctx_count * 2,)),
        ],
        compiler_params=kernel_params(),
        name="attention_backward",
    )(*pieces, out_weight, weight, qkv, x_all, cosine, sine, ids_row, ids_column)


def assemble(pieces, source, shape):
    seqs, ctx_count, rows, width = shape
    count = len(pieces)

    def body(*refs):
        piece_refs, out_ref, sems = refs[:count], refs[count], refs[count + 1]
        copies = plane_copies(piece_refs, source, out_ref, sems, 2, ctx_count)
        for group in copies:
            for copy in group:
                copy.start()
        for group in copies:
            for copy in group:
                copy.wait()

    return pl.pallas_call(
        body,
        out_shape=jax.ShapeDtypeStruct((seqs, ctx_count * rows, width), jnp.bfloat16),
        in_specs=[pl.BlockSpec(memory_space=pl.ANY)] * count,
        out_specs=pl.BlockSpec(memory_space=pl.ANY),
        scratch_shapes=[pltpu.SemaphoreType.DMA((seqs * ctx_count * 2,))],
        name="assemble_rows",
    )(*pieces).reshape(-1, width)


def reduce_pieces(make_piece):
    sent_far = flip(
        jnp.stack([make_piece(1), make_piece(3)]).astype(jnp.bfloat16), "dp", 1
    ).astype(jnp.float32)
    far = make_piece(2) + sent_far[1]
    own = make_piece(0) + sent_far[0]
    return own + flip(far.astype(jnp.bfloat16), "dp", 2).astype(jnp.float32)


def plane_device(
    tokens,
    cotangent,
    rope_positions,
    block_order,
    w_query,
    key_weight,
    value_weight,
    w_out,
    w_gate,
    w_up,
    w_down,
    attn_gain,
    mlp_gain,
):
    f32, b16 = jnp.float32, jnp.bfloat16
    rows, width = tokens.shape[1:]
    block_size = rows // 2
    ctx_count = lax.axis_size("ctx")
    shards = lax.axis_size("fsdp")
    planes = lax.axis_size("dp")
    ctx_rank = lax.axis_index("ctx")
    shard = lax.axis_index("fsdp")
    plane = lax.axis_index("dp")
    heads = QUERY_HEADS // (shards * ctx_count)
    packed = heads * HEAD_SIZE
    lanes = -(-HEAD_SIZE // 128) * 128
    seq_rows = ctx_count * rows

    gains = gather_rows(jnp.stack([attn_gain, mlp_gain]))
    gains = jnp.stack(gains)
    gains = jnp.concatenate(
        [lax.dynamic_index_in_dim(gains, shard ^ j, 0, keepdims=False) for j in range(shards)],
        axis=1,
    ).astype(f32)
    first_gain, second_gain = gains[0], gains[1]
    pos = jnp.stack([rope_positions, flip(rope_positions, "ctx", 1)], axis=1)

    half = rows // 2
    x_pieces, source = gather_plane(tokens[0, :half], tokens[0, half:])

    def columns(weight, relative):
        size = weight.shape[1] // (shards * ctx_count)
        start = ((shard ^ relative) * ctx_count + ctx_rank) * size
        return lax.dynamic_slice_in_dim(weight, start, size, 1)

    def exchange(make):
        return place(
            [
                make(k) if k == 0 else flip(make(k), "fsdp", k)
                for k in range(shards)
            ],
            shard,
        )

    def qkv_columns(k):
        parts = [columns(w, k) for w in (w_query, key_weight, value_weight)]
        joined = jnp.concatenate(parts, axis=1).reshape(w_query.shape[0], heads + 2, HEAD_SIZE)
        return jnp.pad(joined, ((0, 0), (0, 0), (0, lanes - HEAD_SIZE))).reshape(
            w_query.shape[0], -1
        )

    qkv_weight = exchange(qkv_columns)
    out_rows = w_out.shape[0] // ctx_count
    own_out = lax.dynamic_slice_in_dim(w_out, ctx_rank * out_rows, out_rows, 0)
    other_out = lax.dynamic_slice_in_dim(w_out, (1 - ctx_rank) * out_rows, out_rows, 0)
    out_parts = gather_rows(jnp.concatenate([own_out, other_out], axis=0))
    glu_weight = exchange(
        lambda k: jnp.concatenate([columns(w_gate, k), columns(w_up, k)], axis=1)
    )
    c_pieces, unused = gather_plane(cotangent[0, :half], cotangent[0, half:])
    cot_all = assemble(c_pieces, source, (shards, ctx_count, rows, width))
    down_rows = w_down.shape[0] // ctx_count
    own_down = lax.dynamic_slice_in_dim(w_down, ctx_rank * down_rows, down_rows, 0)
    padded_out = jnp.pad(
        own_out.reshape(heads, HEAD_SIZE, width), ((0, 0), (0, lanes - HEAD_SIZE), (0, 0))
    ).reshape(heads * lanes, width)

    pos = jnp.stack(
        [lax.dynamic_index_in_dim(pos, shard ^ j, 0, keepdims=False) for j in range(shards)]
    )
    cosine_table, sine_table = rope_tables(pos.reshape(-1))
    filler = jnp.zeros((cosine_table.shape[0], lanes - HEAD_SIZE), f32)
    cosine = jnp.concatenate([cosine_table, cosine_table, filler], axis=1)
    sine = jnp.concatenate([-sine_table, sine_table, filler], axis=1)
    own_ids = jnp.arange(rows, dtype=jnp.int32)
    seq_tokens = jnp.concatenate(
        [
            token_lookup(block_order, (ctx_rank ^ k) * rows + own_ids, block_size, rows)
            for k in range(ctx_count)
        ]
    )
    ids_row, ids_column = seq_tokens[None, :], seq_tokens[:, None]

    shape = (shards, ctx_count, rows, width, heads)
    x_all, normed_first, qkv, att_low, att_high = attention_forward(
        x_pieces, source, first_gain[None], qkv_weight, cosine, sine, ids_row, ids_column, shape
    )
    a_pieces, unused = gather_plane(att_low, att_high)
    (hidden, normed_second, grad_glu, activated, second_part, keep, send, mlp_keep, mlp_send) = (
        feed_forward(
            x_all,
            a_pieces,
            source,
            out_parts,
            second_gain[None],
            glu_weight,
            own_down,
            cot_all,
            (shards, ctx_count, rows, width, packed),
        )
    )
    ff_width = activated.shape[1]
    grad_normed = scatter_plane(keep, send)
    own_unit2, own_root2 = normalize(hidden)
    grad_hidden, unused = norm_back(grad_normed, own_unit2, own_root2, second_gain)
    grad_hidden = grad_hidden + cotangent[0].astype(f32)
    grad_hidden_b = grad_hidden.astype(b16)
    h_pieces, unused = gather_plane(grad_hidden_b[:half], grad_hidden_b[half:])

    piece = width // planes

    def column_piece(values, j):
        return lax.dynamic_slice_in_dim(values, (plane ^ j) * piece, piece, 1)

    glu_piece = reduce_pieces(lambda j: tn_dot(column_piece(normed_second, j), grad_glu))
    down_piece = reduce_pieces(lambda j: tn_dot(activated, column_piece(cot_all, j)))

    h_all, attended, d_qkv, first_part, keep, send = attention_backward(
        h_pieces,
        source,
        padded_out,
        qkv_weight,
        qkv,
        x_all,
        cosine,
        sine,
        ids_row,
        ids_column,
        shape,
    )
    grad_normed_first = scatter_plane(keep, send)
    own_unit1, own_root1 = normalize(tokens[0].astype(f32))
    grad_input, unused = norm_back(grad_normed_first, own_unit1, own_root1, first_gain)
    grad_input = (grad_hidden + grad_input).astype(b16)

    def compact(value):
        return value.reshape(-1, heads + 2, lanes)[..., :HEAD_SIZE].reshape(value.shape[0], -1)

    out_piece = reduce_pieces(lambda j: tn_dot(attended, column_piece(h_all, j)))
    qkv_piece = reduce_pieces(lambda j: compact(tn_dot(column_piece(normed_first, j), d_qkv)))
    mlp_term = scatter_plane(mlp_keep, mlp_send)
    output = (hidden + mlp_term).astype(b16)

    gain_grads = jnp.concatenate([first_part, second_part], axis=0)
    for axis, bit in (("fsdp", 1), ("ctx", 1), ("dp", 1), ("fsdp", 2), ("dp", 2)):
        gain_grads = gain_grads + flip(gain_grads, axis, bit)
    gain_width = width // (planes * ctx_count * shards)
    gain_at = ((plane * ctx_count + ctx_rank) * shards + shard) * gain_width
    gain_grads = lax.dynamic_slice_in_dim(gain_grads, gain_at, gain_width, 1)

    def swap_rows(value):
        part = value.shape[0] // ctx_count
        kept = lax.dynamic_slice_in_dim(value, ctx_rank * part, part, 0)
        give = lax.dynamic_slice_in_dim(value, (1 - ctx_rank) * part, part, 0).astype(b16)
        return kept, flip(give, "ctx", 1).astype(f32)

    def pair(kept, got, axis):
        return jnp.where(
            ctx_rank == 0,
            jnp.concatenate([kept, got], axis=axis),
            jnp.concatenate([got, kept], axis=axis),
        )

    def swap_columns(value):
        part = value.shape[1] // ctx_count
        kept = lax.dynamic_slice_in_dim(value, ctx_rank * part, part, 1)
        give = lax.dynamic_slice_in_dim(value, (1 - ctx_rank) * part, part, 1).astype(b16)
        return pair(kept, flip(give, "ctx", 1).astype(f32), 0)

    glu_keep, glu_got = swap_rows(glu_piece)
    qkv_keep, qkv_got = swap_rows(qkv_piece)
    cuts = (0, packed, packed + HEAD_SIZE, packed + 2 * HEAD_SIZE)
    qkv_grads = [
        pair(qkv_keep[:, a:b], qkv_got[:, a:b], 1) for a, b in zip(cuts[:-1], cuts[1:])
    ]
    return (
        output[None],
        grad_input[None],
        qkv_grads[0],
        qkv_grads[1],
        qkv_grads[2],
        swap_columns(out_piece),
        pair(glu_keep[:, :ff_width], glu_got[:, :ff_width], 1),
        pair(glu_keep[:, ff_width:], glu_got[:, ff_width:], 1),
        swap_columns(down_piece),
        gain_grads[0],
        gain_grads[1],
    )


def plane_fits(mesh):
    sizes = mesh.shape
    return (
        sizes["ctx"] == 2
        and sizes["fsdp"] == 4
        and sizes["dp"] == 4
        and KEY_VALUE_HEADS == sizes["ctx"] * sizes["fsdp"]
    )


def solution(mesh):
    placed = (
        P(("dp", "fsdp"), "ctx", None),
        P(("dp", "fsdp"), "ctx", None),
        P("dp", "ctx"),
        P(),
        P("fsdp", None),
        P("fsdp", None),
        P("fsdp", None),
        P("fsdp", None),
        P("fsdp", None),
        P("fsdp", None),
        P("fsdp", None),
        P("fsdp"),
        P("fsdp"),
    )
    return jax.shard_map(
        plane_device if plane_fits(mesh) else per_device,
        mesh=mesh,
        in_specs=placed,
        out_specs=(
            P(("dp", "fsdp"), "ctx", None),
            P(("dp", "fsdp"), "ctx", None),
            P(("dp", "ctx"), "fsdp"),
            P(("dp", "ctx"), "fsdp"),
            P(("dp", "ctx"), "fsdp"),
            P("fsdp", ("dp", "ctx")),
            P(("dp", "ctx"), "fsdp"),
            P(("dp", "ctx"), "fsdp"),
            P("fsdp", ("dp", "ctx")),
            P(("dp", "ctx", "fsdp")),
            P(("dp", "ctx", "fsdp")),
        ),
        check_vma=False,
    )
```

```python
import jax
import jax.numpy as jnp
from jax import lax
from jax.experimental import pallas as pl
from jax.experimental.pallas import tpu as pltpu
from jax.sharding import PartitionSpec as P

QUERY_HEADS = 16
KEY_VALUE_HEADS = 8
HEAD_SIZE = 96


rope_base = 100000.0
norm_eps = 1e-05
masked_score = -1e30


def matrix_product(left, right):
    return jnp.dot(left, right, preferred_element_type=jnp.float32)


def back_mul(left, right):
    return lax.dot_general(
        left, right, (((left.ndim - 1,), (1,)), ((), ())), preferred_element_type=jnp.float32
    )


def weight_term(left, right):
    return lax.dot_general(
        left, right, (((0, 1), (0, 1)), ((), ())), preferred_element_type=jnp.float32
    )


def rope_tables(positions):
    half_dim = HEAD_SIZE // 2
    inverse = rope_base ** (-2.0 * jnp.arange(half_dim, dtype=jnp.float32) / HEAD_SIZE)
    angles = positions.astype(jnp.float32)[..., None] * inverse
    return (jnp.cos(angles), jnp.sin(angles))


def apply_rotary(values, cosine_table, sine_table, direction):
    leading = values.shape[:-1]
    head_count = values.shape[-1] // HEAD_SIZE
    half_dim = HEAD_SIZE // 2
    halves = values.reshape(leading + (head_count, 2, half_dim))
    first_half = halves[..., 0, :]
    second_half = halves[..., 1, :]
    cos_part = cosine_table[..., None, :]
    sin_part = direction * sine_table[..., None, :]
    joined = jnp.stack(
        [
            first_half * cos_part - second_half * sin_part,
            second_half * cos_part + first_half * sin_part,
        ],
        axis=-2,
    )
    return joined.reshape(leading + (head_count * HEAD_SIZE,))


def normalize(values):
    inv_root = lax.rsqrt(jnp.mean(values * values, axis=-1, keepdims=True) + norm_eps)
    return (values * inv_root, inv_root)


def norm_back(grad_output, unit_rows, inv_root, gain_vec):
    grad_unit = grad_output * gain_vec
    grad_gain = jnp.sum(grad_output * unit_rows, axis=0)
    grad_input = inv_root * (
        grad_unit - unit_rows * jnp.mean(grad_unit * unit_rows, axis=-1, keepdims=True)
    )
    return (grad_input, grad_gain)


def token_lookup(block_order, row_ids, block_size, local_rows):
    slot_ids = 2 * (row_ids // local_rows) + row_ids % local_rows // block_size
    onehot_table = (
        slot_ids[:, None] == jnp.arange(block_order.shape[0], dtype=jnp.int32)[None, :]
    ).astype(jnp.int32)
    chosen = jnp.sum(onehot_table * block_order[None, :], axis=1)
    return chosen * block_size + row_ids % block_size


def attend_forward(query_matrix, key_stack, value_stack, own_tokens, token_stack):
    seq_count = query_matrix.shape[0]
    count_of_rows = query_matrix.shape[1]
    kv_heads = key_stack.shape[-1] // HEAD_SIZE
    query_group_width = QUERY_HEADS // KEY_VALUE_HEADS
    score_scale = HEAD_SIZE ** (-0.5)
    head_queries = query_matrix.reshape(
        seq_count, count_of_rows, kv_heads, query_group_width, HEAD_SIZE
    )

    def absorb(state, block_in):
        running_max, running_sum, weighted = state
        piece_keys, piece_values, piece_tokens = block_in
        piece_rows = piece_keys.shape[1]
        scores = (
            jnp.einsum(
                "sqngd,sknd->sngqk",
                head_queries,
                piece_keys.reshape(seq_count, piece_rows, kv_heads, HEAD_SIZE),
                preferred_element_type=jnp.float32,
            )
            * score_scale
        )
        allowed = piece_tokens[None, None, None, None, :] <= own_tokens[None, None, None, :, None]
        scores = jnp.where(allowed, scores, masked_score)
        new_max = jnp.maximum(running_max, jnp.max(scores, axis=-1))
        weights_now = jnp.where(allowed, jnp.exp(scores - new_max[..., None]), 0.0)
        decay_factor = jnp.exp(running_max - new_max)
        new_sum = running_sum * decay_factor + jnp.sum(weights_now, axis=-1)
        block_sum = jnp.einsum(
            "sngqk,sknd->sngqd",
            weights_now.astype(jnp.bfloat16),
            piece_values.reshape(seq_count, piece_rows, kv_heads, HEAD_SIZE),
            preferred_element_type=jnp.float32,
        )
        return ((new_max, new_sum, weighted * decay_factor[..., None] + block_sum), 0)

    stat_shape = (seq_count, kv_heads, query_group_width, count_of_rows)
    start_state = (
        jnp.full(stat_shape, masked_score, jnp.float32),
        jnp.zeros(stat_shape, jnp.float32),
        jnp.zeros(stat_shape + (HEAD_SIZE,), jnp.float32),
    )
    (running_max, running_sum, weighted), unused = lax.scan(
        absorb, start_state, (key_stack, value_stack, token_stack)
    )
    attended_output = (
        jnp.transpose(weighted / running_sum[..., None], (0, 3, 1, 2, 4))
        .reshape(seq_count, count_of_rows, kv_heads * query_group_width * HEAD_SIZE)
        .astype(jnp.bfloat16)
    )
    return (attended_output, running_max + jnp.log(running_sum))


def attend_backward(
    query_matrix,
    attended_gradient,
    attended_output,
    log_sums,
    own_tokens,
    key_stack,
    value_stack,
    token_stack,
):
    seq_count = query_matrix.shape[0]
    count_of_rows = query_matrix.shape[1]
    kv_heads = key_stack.shape[-1] // HEAD_SIZE
    query_group_width = QUERY_HEADS // KEY_VALUE_HEADS
    score_scale = HEAD_SIZE ** (-0.5)
    head_queries = query_matrix.reshape(
        seq_count, count_of_rows, kv_heads, query_group_width, HEAD_SIZE
    )
    head_gradient = attended_gradient.reshape(
        seq_count, count_of_rows, kv_heads, query_group_width, HEAD_SIZE
    )
    head_outputs = attended_output.astype(jnp.float32).reshape(
        seq_count, count_of_rows, kv_heads, query_group_width, HEAD_SIZE
    )
    row_delta = jnp.transpose(
        jnp.sum(head_gradient.astype(jnp.float32) * head_outputs, axis=-1), (0, 2, 3, 1)
    )

    def key_step(grad_query_sum, block_in):
        piece_keys, piece_values, piece_tokens = block_in
        piece_rows = piece_keys.shape[1]
        head_keys = piece_keys.reshape(seq_count, piece_rows, kv_heads, HEAD_SIZE)
        head_values = piece_values.reshape(seq_count, piece_rows, kv_heads, HEAD_SIZE)
        scores = (
            jnp.einsum(
                "sqngd,sknd->sngqk", head_queries, head_keys, preferred_element_type=jnp.float32
            )
            * score_scale
        )
        allowed = piece_tokens[None, None, None, None, :] <= own_tokens[None, None, None, :, None]
        scores = jnp.where(allowed, scores, masked_score)
        attn_prob = jnp.where(allowed, jnp.exp(scores - log_sums[..., None]), 0.0)
        grad_prob = jnp.einsum(
            "sqngd,sknd->sngqk", head_gradient, head_values, preferred_element_type=jnp.float32
        )
        grad_scores = (attn_prob * (grad_prob - row_delta[..., None]) * score_scale).astype(
            jnp.bfloat16
        )
        grad_value_piece = jnp.einsum(
            "sngqk,sqngd->sknd",
            attn_prob.astype(jnp.bfloat16),
            head_gradient,
            preferred_element_type=jnp.float32,
        )
        grad_key_piece = jnp.einsum(
            "sngqk,sqngd->sknd", grad_scores, head_queries, preferred_element_type=jnp.float32
        )
        grad_query_sum = grad_query_sum + jnp.einsum(
            "sngqk,sknd->sqngd", grad_scores, head_keys, preferred_element_type=jnp.float32
        )
        return (
            grad_query_sum,
            (
                grad_key_piece.reshape(seq_count, piece_rows, kv_heads * HEAD_SIZE),
                grad_value_piece.reshape(seq_count, piece_rows, kv_heads * HEAD_SIZE),
            ),
        )

    zero_query = jnp.zeros(
        (seq_count, count_of_rows, kv_heads, query_group_width, HEAD_SIZE), jnp.float32
    )
    grad_query_sum, (key_pieces, value_pieces) = lax.scan(
        key_step, zero_query, (key_stack, value_stack, token_stack)
    )
    return (
        grad_query_sum.reshape(seq_count, count_of_rows, kv_heads * query_group_width * HEAD_SIZE),
        key_pieces,
        value_pieces,
    )


def per_device(
    tokens,
    cotangent,
    rope_positions,
    block_order,
    w_query,
    key_weight,
    value_weight,
    w_out,
    w_gate,
    w_up,
    w_down,
    attn_gain,
    mlp_gain,
):
    local_rows = tokens.shape[1]
    block_size = local_rows // 2
    ctx_count = lax.axis_size("ctx")
    ctx_rank = lax.axis_index("ctx")
    shard_rank = lax.axis_index("fsdp")
    outer_count = lax.axis_size("dp") * ctx_count
    own_tokens = token_lookup(
        block_order,
        ctx_rank * local_rows + jnp.arange(local_rows, dtype=jnp.int32),
        block_size,
        local_rows,
    )
    token_stack = token_lookup(
        block_order, jnp.arange(ctx_count * local_rows, dtype=jnp.int32), block_size, local_rows
    ).reshape(ctx_count, local_rows)
    residual_in = tokens[0].astype(jnp.float32)
    grad_out = cotangent[0]
    gathered = (
        lax.all_gather(w_query, "fsdp", axis=0, tiled=True),
        lax.all_gather(key_weight, "fsdp", axis=0, tiled=True),
        lax.all_gather(value_weight, "fsdp", axis=0, tiled=True),
        lax.all_gather(w_out, "fsdp", axis=0, tiled=True),
        lax.all_gather(w_gate, "fsdp", axis=0, tiled=True),
        lax.all_gather(w_up, "fsdp", axis=0, tiled=True),
        lax.all_gather(w_down, "fsdp", axis=0, tiled=True),
        lax.all_gather(attn_gain, "fsdp", axis=0, tiled=True),
        lax.all_gather(mlp_gain, "fsdp", axis=0, tiled=True),
    )
    part_query, part_key, part_value, part_out, part_gate, part_up, part_down = (
        gathered[0],
        gathered[1],
        gathered[2],
        gathered[3],
        gathered[4],
        gathered[5],
        gathered[6],
    )
    first_gain = gathered[7].astype(jnp.float32)
    second_gain = gathered[8].astype(jnp.float32)
    positions = lax.dynamic_slice_in_dim(rope_positions, shard_rank, 1, 0)
    unit_first, root_first = normalize(residual_in)
    first_normed_input = (unit_first * first_gain).astype(jnp.bfloat16)
    normed_rows = first_normed_input[None]
    cosine_table, sine_table = rope_tables(positions)
    query_matrix = apply_rotary(
        matrix_product(normed_rows, part_query), cosine_table, sine_table, 1.0
    ).astype(jnp.bfloat16)
    rotated_keys = apply_rotary(
        matrix_product(normed_rows, part_key), cosine_table, sine_table, 1.0
    ).astype(jnp.bfloat16)
    every_value = matrix_product(normed_rows, part_value).astype(jnp.bfloat16)
    key_stack, value_stack = (
        lax.all_gather(rotated_keys[None], "ctx", axis=0, tiled=True),
        lax.all_gather(every_value[None], "ctx", axis=0, tiled=True),
    )
    attended_output, log_sums = attend_forward(
        query_matrix, key_stack, value_stack, own_tokens, token_stack
    )
    attn_term = matrix_product(attended_output[0], part_out)
    hidden_res = residual_in + attn_term
    unit_second, root_second = normalize(hidden_res)
    normed_second = (unit_second * second_gain).astype(jnp.bfloat16)
    mlp_input, cot_rows = (normed_second[None], cotangent)
    gate_pre = matrix_product(mlp_input, part_gate)
    up_pre = matrix_product(mlp_input, part_up)
    sigmoid_gate = jax.nn.sigmoid(gate_pre)
    silu_gate = gate_pre * sigmoid_gate
    activated = (silu_gate * up_pre).astype(jnp.bfloat16)
    mlp_term = matrix_product(activated[0], part_down)
    output = (hidden_res + mlp_term).astype(jnp.bfloat16)
    grad_act = back_mul(cot_rows, part_down)
    grad_gate_pre = (
        grad_act * up_pre * sigmoid_gate * (1.0 + gate_pre * (1.0 - sigmoid_gate))
    ).astype(jnp.bfloat16)
    grad_up_pre = (grad_act * silu_gate).astype(jnp.bfloat16)
    grad_gate = weight_term(mlp_input, grad_gate_pre)
    grad_up = weight_term(mlp_input, grad_up_pre)
    grad_down_t = weight_term(cot_rows, activated)
    grad_normed = back_mul(grad_gate_pre[0], part_gate) + back_mul(grad_up_pre[0], part_up)
    grad_hidden, grad_second_gain = norm_back(grad_normed, unit_second, root_second, second_gain)
    grad_hidden = grad_hidden + grad_out.astype(jnp.float32)
    grad_hidden_b = grad_hidden.astype(jnp.bfloat16)
    back_input = grad_hidden_b[None]
    grad_out_t = weight_term(back_input, attended_output)
    attended_gradient = back_mul(back_input, part_out).astype(jnp.bfloat16)
    grad_query_sum, key_pieces, value_pieces = attend_backward(
        query_matrix,
        attended_gradient,
        attended_output,
        log_sums,
        own_tokens,
        key_stack,
        value_stack,
        token_stack,
    )
    key_sum, value_sum = (
        lax.psum_scatter(
            key_pieces.astype(jnp.bfloat16), "ctx", scatter_dimension=0, tiled=True
        ).astype(jnp.float32),
        lax.psum_scatter(
            value_pieces.astype(jnp.bfloat16), "ctx", scatter_dimension=0, tiled=True
        ).astype(jnp.float32),
    )
    grad_queries = apply_rotary(grad_query_sum, cosine_table, sine_table, -1.0).astype(jnp.bfloat16)
    key_gradient_b = apply_rotary(key_sum[0], cosine_table, sine_table, -1.0).astype(jnp.bfloat16)
    value_gradient_b = value_sum[0].astype(jnp.bfloat16)
    grad_wq = weight_term(normed_rows, grad_queries)
    grad_wk = weight_term(normed_rows, key_gradient_b)
    grad_wv = weight_term(normed_rows, value_gradient_b)
    grad_normed_first = (
        back_mul(grad_queries[0], part_query)
        + back_mul(key_gradient_b[0], part_key)
        + back_mul(value_gradient_b[0], part_value)
    )
    grad_input, grad_first_gain = norm_back(grad_normed_first, unit_first, root_first, first_gain)
    grad_input = (grad_hidden + grad_input).astype(jnp.bfloat16)
    gain_first = grad_first_gain.reshape(outer_count, -1)
    gain_second = grad_second_gain.reshape(outer_count, -1)
    summed = (
        lax.psum_scatter(
            grad_wq.astype(jnp.bfloat16), "fsdp", scatter_dimension=1, tiled=True
        ).astype(jnp.float32),
        lax.psum_scatter(
            grad_wk.astype(jnp.bfloat16), "fsdp", scatter_dimension=1, tiled=True
        ).astype(jnp.float32),
        lax.psum_scatter(
            grad_wv.astype(jnp.bfloat16), "fsdp", scatter_dimension=1, tiled=True
        ).astype(jnp.float32),
        lax.psum_scatter(
            grad_out_t.astype(jnp.bfloat16), "fsdp", scatter_dimension=1, tiled=True
        ).astype(jnp.float32),
        lax.psum_scatter(
            grad_gate.astype(jnp.bfloat16), "fsdp", scatter_dimension=1, tiled=True
        ).astype(jnp.float32),
        lax.psum_scatter(
            grad_up.astype(jnp.bfloat16), "fsdp", scatter_dimension=1, tiled=True
        ).astype(jnp.float32),
        lax.psum_scatter(
            grad_down_t.astype(jnp.bfloat16), "fsdp", scatter_dimension=1, tiled=True
        ).astype(jnp.float32),
        lax.psum_scatter(
            gain_first.astype(jnp.bfloat16), "fsdp", scatter_dimension=1, tiled=True
        ).astype(jnp.float32),
        lax.psum_scatter(
            gain_second.astype(jnp.bfloat16), "fsdp", scatter_dimension=1, tiled=True
        ).astype(jnp.float32),
    )
    col_query, col_key, col_value, col_out, col_gate, col_up, col_down = (
        summed[0],
        summed[1],
        summed[2],
        summed[3],
        summed[4],
        summed[5],
        summed[6],
    )
    gain_first, gain_second = (summed[7], summed[8])
    reduced = (
        lax.psum_scatter(
            col_query.astype(jnp.bfloat16), ("dp", "ctx"), scatter_dimension=0, tiled=True
        ).astype(jnp.float32),
        lax.psum_scatter(
            col_key.astype(jnp.bfloat16), ("dp", "ctx"), scatter_dimension=0, tiled=True
        ).astype(jnp.float32),
        lax.psum_scatter(
            col_value.astype(jnp.bfloat16), ("dp", "ctx"), scatter_dimension=0, tiled=True
        ).astype(jnp.float32),
        lax.psum_scatter(
            col_out.astype(jnp.bfloat16), ("dp", "ctx"), scatter_dimension=0, tiled=True
        ).astype(jnp.float32),
        lax.psum_scatter(
            col_gate.astype(jnp.bfloat16), ("dp", "ctx"), scatter_dimension=0, tiled=True
        ).astype(jnp.float32),
        lax.psum_scatter(
            col_up.astype(jnp.bfloat16), ("dp", "ctx"), scatter_dimension=0, tiled=True
        ).astype(jnp.float32),
        lax.psum_scatter(
            col_down.astype(jnp.bfloat16), ("dp", "ctx"), scatter_dimension=0, tiled=True
        ).astype(jnp.float32),
        lax.psum_scatter(
            gain_first.astype(jnp.bfloat16), ("dp", "ctx"), scatter_dimension=0, tiled=True
        ).astype(jnp.float32),
        lax.psum_scatter(
            gain_second.astype(jnp.bfloat16), ("dp", "ctx"), scatter_dimension=0, tiled=True
        ).astype(jnp.float32),
    )
    return (
        output[None],
        grad_input[None],
        reduced[0],
        reduced[1],
        reduced[2],
        reduced[3].T,
        reduced[4],
        reduced[5],
        reduced[6].T,
        reduced[7].reshape(-1),
        reduced[8].reshape(-1),
    )


def flip(values, axis, bit):
    size = lax.axis_size(axis)
    return lax.ppermute(values, axis, [(i, i ^ bit) for i in range(size)])


def after(value, *others):
    return lax.optimization_barrier((value,) + others)[0]


def gather_plane(own):
    x_block = flip(own, "ctx", 1)
    y_block = flip(own, "fsdp", 2)
    own_core = flip(own, "fsdp", 1)
    low_far = flip(x_block[:1], "fsdp", 2)
    high_far = flip(y_block[1:], "ctx", 1)
    near = [own, x_block, y_block, low_far, high_far]
    arrays = near + [own_core] + [flip(v, "fsdp", 1) for v in near[1:]]
    source = {}
    for core in range(2):
        for half in range(2):
            source[0, 0, core, half] = (5 * core, half)
            source[1, 0, core, half] = (5 * core + 1, half)
            source[0, 1, core, half] = (5 * core + 2, half)
            source[1, 1, core, half] = (5 * core + 3 + half, 0)
    return arrays, source


def scatter_plane(keep, send):
    f32, b16 = jnp.float32, jnp.bfloat16
    both = keep.astype(f32) + flip(send, "fsdp", 1).astype(f32)
    half = both.shape[2] // 2
    low, high = both[:, :, :half], both[:, :, half:]
    low_got = flip(low[1].astype(b16), "fsdp", 2)
    high_got = flip(high[:, 1].astype(b16), "ctx", 1)
    low = low[0] + low_got.astype(f32)
    high = high[:, 0] + high_got.astype(f32)
    low_got = flip(low[1].astype(b16), "ctx", 1)
    high_got = flip(high[1].astype(b16), "fsdp", 2)
    return jnp.concatenate(
        [low[0] + low_got.astype(f32), high[0] + high_got.astype(f32)], axis=0
    )


def gather_rows(own):
    across = flip(own, "fsdp", 2)
    return [own, flip(own, "fsdp", 1), across, flip(across, "fsdp", 1)]


def kernel_params():
    return pltpu.CompilerParams(
        vmem_limit_bytes=56 * 1024 * 1024, dimension_semantics=("arbitrary",)
    )


def whole(shape):
    return pl.BlockSpec(shape, lambda s: (0,) * len(shape))


def place(parts, starts, total_rows, shard, plane):
    width = parts[0].shape[1]
    count = len(parts)

    def body(shard_ref, plane_ref, *refs):
        ins, out, sems = refs[:count], refs[count], refs[count + 1]
        copies = []
        for k in range(count):
            rows = parts[k].shape[0]
            start = pl.multiple_of(starts[k](shard_ref[0], plane_ref[0]), rows)
            copies.append(
                pltpu.make_async_copy(ins[k], out.at[pl.ds(start, rows)], sems.at[k])
            )
        for copy in copies:
            copy.start()
        for copy in copies:
            copy.wait()

    return pl.pallas_call(
        body,
        out_shape=jax.ShapeDtypeStruct((total_rows, width), parts[0].dtype),
        in_specs=[pl.BlockSpec(memory_space=pltpu.SMEM)] * 2
        + [pl.BlockSpec(memory_space=pl.ANY)] * count,
        out_specs=pl.BlockSpec(memory_space=pltpu.VMEM),
        scratch_shapes=[pltpu.SemaphoreType.DMA((count,))],
        compiler_params=pltpu.CompilerParams(vmem_limit_bytes=24 * 1024 * 1024),
        name="place_rows",
    )(shard.reshape(1), plane.reshape(1), *parts)


def plane_copies(refs, source, scratch, sems, core_count, ctx_count):
    copies = []
    count = 0
    for j in range(scratch.shape[0]):
        group = []
        for k in range(ctx_count):
            for half in range(2):
                at, lead = source[k, j // core_count, j % core_count, half]
                rows = refs[at].shape[1]
                start = (k * 2 + half) * rows
                group.append(
                    pltpu.make_async_copy(
                        refs[at].at[lead], scratch.at[j, pl.ds(start, rows)], sems.at[count]
                    )
                )
                count += 1
        copies.append(group)
    return copies


def arrive(copies, step):
    @pl.when(step == 0)
    def _():
        for group in copies:
            for copy in group:
                copy.start()

    for j, group in enumerate(copies):

        @pl.when(step == j)
        def _():
            for copy in group:
                copy.wait()


def swap_halves(value):
    half = HEAD_SIZE // 2
    lane = lax.broadcasted_iota(jnp.int32, value.shape, 1)
    lanes = value.shape[1]
    return jnp.where(
        lane < half, pltpu.roll(value, lanes - half, 1), pltpu.roll(value, half, 1)
    )


def widen(value, lanes):
    fill = jnp.zeros((value.shape[0], lanes - value.shape[1]), value.dtype)
    return jnp.concatenate([value, fill], axis=1)


def nt_dot(left, right):
    return lax.dot_general(
        left, right, (((1,), (1,)), ((), ())), preferred_element_type=jnp.float32
    )


def tn_dot(left, right):
    return lax.dot_general(
        left, right, (((0,), (0,)), ((), ())), preferred_element_type=jnp.float32
    )


def head_probs(query, key, allowed):
    scores = nt_dot(query, key) * (HEAD_SIZE ** (-0.5))
    scores = jnp.where(allowed, scores, masked_score)
    row_max = jnp.max(scores, axis=-1, keepdims=True)
    weights_now = jnp.where(allowed, jnp.exp(scores - row_max), 0.0)
    return weights_now / jnp.sum(weights_now, axis=-1, keepdims=True)


def attention_forward(pieces, source, gain, weight, cosine, sine, ids_row, ids_column, shape):
    seqs, ctx_count, rows, width, heads = shape
    f32, b16 = jnp.float32, jnp.bfloat16
    seq_rows = ctx_count * rows
    lanes = cosine.shape[1]
    packed = heads * HEAD_SIZE
    count = len(pieces)

    def body(*refs):
        piece_refs = refs[:count]
        gain_ref, w_ref, cos_ref, sin_ref, row_ref, col_ref = refs[count : count + 6]
        all_ref, normed_ref, qkv_ref, att_ref, x_ref, sems = refs[count + 6 :]
        step = pl.program_id(0)
        arrive(plane_copies(piece_refs, source, x_ref, sems, 2, ctx_count), step)
        raw = x_ref[step]
        all_ref[...] = raw
        value = raw.astype(f32)
        root = lax.rsqrt(jnp.mean(value * value, axis=-1, keepdims=True) + norm_eps)
        normed = (value * root * gain_ref[...]).astype(b16)
        normed_ref[...] = normed
        qkv = jnp.dot(normed, w_ref[...], preferred_element_type=f32)
        cos, sin = cos_ref[...], sin_ref[...]
        allowed = row_ref[...] <= col_ref[...]
        parts = []
        for i in range(heads + 2):
            part = widen(qkv[:, i * HEAD_SIZE : (i + 1) * HEAD_SIZE], lanes)
            if i <= heads:
                part = part * cos + swap_halves(part) * sin
            parts.append(part.astype(b16))
            qkv_ref[:, i * lanes : (i + 1) * lanes] = parts[i]
        mixed = []
        for h in range(heads):
            prob = head_probs(parts[h], parts[heads], allowed).astype(b16)
            mixed.append(jnp.dot(prob, parts[heads + 1], preferred_element_type=f32))
        merged = jnp.concatenate([m[:, :HEAD_SIZE] for m in mixed], axis=1).astype(b16)
        att_ref[...] = merged.reshape(ctx_count, 1, rows, packed)

    block = lambda n: pl.BlockSpec((seq_rows, n), lambda s: (s, 0))
    half = pl.BlockSpec((ctx_count, 1, rows, packed), lambda s: (0, s, 0, 0))
    total = seqs * seq_rows
    return pl.pallas_call(
        body,
        grid=(seqs,),
        in_specs=[pl.BlockSpec(memory_space=pl.ANY)] * count
        + [whole((1, width)), whole(weight.shape), block(lanes), block(lanes)]
        + [whole((1, seq_rows)), whole((seq_rows, 1))],
        out_specs=[block(width), block(width), block((heads + 2) * lanes), half],
        out_shape=[
            jax.ShapeDtypeStruct((total, width), b16),
            jax.ShapeDtypeStruct((total, width), b16),
            jax.ShapeDtypeStruct((total, (heads + 2) * lanes), b16),
            jax.ShapeDtypeStruct((ctx_count, seqs, rows, packed), b16),
        ],
        scratch_shapes=[
            pltpu.VMEM((seqs, seq_rows, width), b16),
            pltpu.SemaphoreType.DMA((seqs * ctx_count * 2,)),
        ],
        compiler_params=kernel_params(),
        name="attention_forward",
    )(*pieces, gain, weight, cosine, sine, ids_row, ids_column)


def feed_forward(x_all, pieces, source, out_weight, gain, glu_weight, down, cot_all, shape):
    seqs, ctx_count, rows, width, packed = shape
    f32, b16 = jnp.float32, jnp.bfloat16
    seq_rows = ctx_count * rows
    ff = down.shape[0]
    piece_args, piece_specs = [], []
    for j in range(seqs):
        for k in range(ctx_count):
            for t in range(ctx_count):
                at, lead = source[k, j // 2, j % 2, t ^ k]
                piece_args.append(pieces[at])
                piece_specs.append(
                    pl.BlockSpec(
                        (1, 1, rows, packed), lambda s, j=j, lead=lead: (lead, s ^ j, 0, 0)
                    )
                )
    count = len(piece_args)

    def body(x_ref, *refs):
        piece_refs = refs[:count]
        out_ref, gain_ref, glu_ref, down_ref, cot_ref = refs[count : count + 5]
        (own_ref, normed_ref, grad_ref, act_ref, gain_out, keep_ref, send_ref, mkeep_ref,
         msend_ref) = refs[count + 5 :]
        step = pl.program_id(0)
        hidden = x_ref[...].astype(f32)
        for j in range(seqs):
            for k in range(ctx_count):
                base = (j * ctx_count + k) * ctx_count
                left = jnp.concatenate(
                    [piece_refs[base + t][0, 0] for t in range(ctx_count)], axis=0
                )
                hidden = hidden + jnp.dot(
                    left,
                    out_ref[(j * ctx_count + k) * packed : (j * ctx_count + k + 1) * packed],
                    preferred_element_type=f32,
                )

        @pl.when(step == 0)
        def _():
            own_ref[...] = hidden[:rows]
            gain_out[...] = jnp.zeros(gain_out.shape, f32)

        root = lax.rsqrt(jnp.mean(hidden * hidden, axis=-1, keepdims=True) + norm_eps)
        unit = hidden * root
        normed = (unit * gain_ref[...]).astype(b16)
        normed_ref[...] = normed
        gate = jnp.dot(normed, glu_ref[:, :ff], preferred_element_type=f32)
        up = jnp.dot(normed, glu_ref[:, ff:], preferred_element_type=f32)
        grad_act = nt_dot(cot_ref[...], down_ref[...])
        sig = jax.nn.sigmoid(gate)
        silu = gate * sig
        act = (silu * up).astype(b16)
        act_ref[...] = act
        grad_gate = (grad_act * up * sig * (1.0 + gate * (1.0 - sig))).astype(b16)
        grad_up = (grad_act * silu).astype(b16)
        grad_ref[:, :ff] = grad_gate
        grad_ref[:, ff:] = grad_up
        back = nt_dot(grad_gate, glu_ref[:, :ff]) + nt_dot(grad_up, glu_ref[:, ff:])
        gain_out[...] += jnp.sum(back * unit, axis=0, keepdims=True)
        mixed = jnp.dot(act, down_ref[...], preferred_element_type=f32)
        back = back.astype(b16).reshape(1, ctx_count, rows, width)
        mixed = mixed.astype(b16).reshape(1, ctx_count, rows, width)

        @pl.when(step % 2 == 0)
        def _():
            keep_ref[...] = back
            mkeep_ref[...] = mixed

        @pl.when(step % 2 == 1)
        def _():
            send_ref[...] = back
            msend_ref[...] = mixed

    block = lambda n: pl.BlockSpec((seq_rows, n), lambda s: (s, 0))
    paired = pl.BlockSpec((1, ctx_count, rows, width), lambda s: (s // 2, 0, 0, 0))
    total = seqs * seq_rows
    pair_shape = jax.ShapeDtypeStruct((seqs // 2, ctx_count, rows, width), b16)
    return pl.pallas_call(
        body,
        grid=(seqs,),
        in_specs=[block(width)]
        + piece_specs
        + [whole(out_weight.shape), whole((1, width)), whole(glu_weight.shape), whole(down.shape), block(width)],
        out_specs=[whole((rows, width)), block(width), block(2 * ff), block(ff), whole((1, width))]
        + [paired] * 4,
        out_shape=[
            jax.ShapeDtypeStruct((rows, width), f32),
            jax.ShapeDtypeStruct((total, width), b16),
            jax.ShapeDtypeStruct((total, 2 * ff), b16),
            jax.ShapeDtypeStruct((total, ff), b16),
            jax.ShapeDtypeStruct((1, width), f32),
        ]
        + [pair_shape] * 4,
        compiler_params=kernel_params(),
        name="feed_forward",
    )(x_all, *piece_args, out_weight, gain, glu_weight, down, cot_all)


def attention_backward(
    pieces, source, out_weight, weight, qkv, x_all, cosine, sine, ids_row, ids_column, shape
):
    seqs, ctx_count, rows, width, heads = shape
    f32, b16 = jnp.float32, jnp.bfloat16
    seq_rows = ctx_count * rows
    lanes = cosine.shape[1]
    packed = heads * HEAD_SIZE
    count = len(pieces)
    score_scale = HEAD_SIZE ** (-0.5)

    def body(*refs):
        piece_refs = refs[:count]
        out_ref, w_ref, qkv_ref, xin_ref, cos_ref, sin_ref, row_ref, col_ref = refs[
            count : count + 8
        ]
        all_ref, att_ref, d_ref, gain_out, keep_ref, send_ref, h_ref, sems = refs[count + 8 :]
        step = pl.program_id(0)
        arrive(plane_copies(piece_refs, source, h_ref, sems, 2, ctx_count), step)
        grad_hidden = h_ref[step]
        all_ref[...] = grad_hidden
        grad_attended = nt_dot(grad_hidden, out_ref[...]).astype(b16)
        cos, sin = cos_ref[...], sin_ref[...]
        allowed = row_ref[...] <= col_ref[...]
        key = qkv_ref[:, heads * lanes : (heads + 1) * lanes]
        value = qkv_ref[:, (heads + 1) * lanes :]
        grad_key, grad_value, mixed, grads = 0.0, 0.0, [], []
        for h in range(heads):
            query = qkv_ref[:, h * lanes : (h + 1) * lanes]
            grad_head = grad_attended[:, h * lanes : (h + 1) * lanes]
            prob = head_probs(query, key, allowed)
            prob_b = prob.astype(b16)
            head_out = jnp.dot(prob_b, value, preferred_element_type=f32).astype(b16)
            mixed.append(head_out[:, :HEAD_SIZE].astype(f32))
            delta = jnp.sum(
                grad_head.astype(f32) * head_out.astype(f32), axis=-1, keepdims=True
            )
            grad_prob = nt_dot(grad_head, value)
            grad_scores = (prob * (grad_prob - delta) * score_scale).astype(b16)
            grad_query = jnp.dot(grad_scores, key, preferred_element_type=f32)
            grads.append(grad_query * cos - swap_halves(grad_query) * sin)
            grad_key = grad_key + tn_dot(grad_scores, query)
            grad_value = grad_value + tn_dot(prob_b, grad_head)
        att_ref[...] = jnp.concatenate(mixed, axis=1).astype(b16)
        grads.append(grad_key * cos - swap_halves(grad_key) * sin)
        grads.append(grad_value)
        joined = jnp.concatenate([g[:, :HEAD_SIZE] for g in grads], axis=1).astype(b16)
        d_ref[...] = joined
        back = nt_dot(joined, w_ref[...])
        x = xin_ref[...].astype(f32)
        unit = x * lax.rsqrt(jnp.mean(x * x, axis=-1, keepdims=True) + norm_eps)

        @pl.when(step == 0)
        def _():
            gain_out[...] = jnp.zeros(gain_out.shape, f32)

        gain_out[...] += jnp.sum(back * unit, axis=0, keepdims=True)
        back = back.astype(b16).reshape(1, ctx_count, rows, width)

        @pl.when(step % 2 == 0)
        def _():
            keep_ref[...] = back

        @pl.when(step % 2 == 1)
        def _():
            send_ref[...] = back

    block = lambda n: pl.BlockSpec((seq_rows, n), lambda s: (s, 0))
    paired = pl.BlockSpec((1, ctx_count, rows, width), lambda s: (s // 2, 0, 0, 0))
    total = seqs * seq_rows
    pair_shape = jax.ShapeDtypeStruct((seqs // 2, ctx_count, rows, width), b16)
    return pl.pallas_call(
        body,
        grid=(seqs,),
        in_specs=[pl.BlockSpec(memory_space=pl.ANY)] * count
        + [whole(out_weight.shape), whole(weight.shape), block(qkv.shape[1]), block(width)]
        + [block(lanes), block(lanes), whole((1, seq_rows)), whole((seq_rows, 1))],
        out_specs=[block(width), block(packed), block(weight.shape[1]), whole((1, width))]
        + [paired] * 2,
        out_shape=[
            jax.ShapeDtypeStruct((total, width), b16),
            jax.ShapeDtypeStruct((total, packed), b16),
            jax.ShapeDtypeStruct((total, weight.shape[1]), b16),
            jax.ShapeDtypeStruct((1, width), f32),
        ]
        + [pair_shape] * 2,
        scratch_shapes=[
            pltpu.VMEM((seqs, seq_rows, width), b16),
            pltpu.SemaphoreType.DMA((seqs * ctx_count * 2,)),
        ],
        compiler_params=kernel_params(),
        name="attention_backward",
    )(*pieces, out_weight, weight, qkv, x_all, cosine, sine, ids_row, ids_column)


def assemble(pieces, source, shape):
    seqs, ctx_count, rows, width = shape
    count = len(pieces)

    def body(*refs):
        piece_refs, out_ref, sems = refs[:count], refs[count], refs[count + 1]
        copies = plane_copies(piece_refs, source, out_ref, sems, 2, ctx_count)
        for group in copies:
            for copy in group:
                copy.start()
        for group in copies:
            for copy in group:
                copy.wait()

    return pl.pallas_call(
        body,
        out_shape=jax.ShapeDtypeStruct((seqs, ctx_count * rows, width), jnp.bfloat16),
        in_specs=[pl.BlockSpec(memory_space=pl.ANY)] * count,
        out_specs=pl.BlockSpec(memory_space=pltpu.VMEM),
        scratch_shapes=[pltpu.SemaphoreType.DMA((seqs * ctx_count * 2,))],
        compiler_params=pltpu.CompilerParams(vmem_limit_bytes=24 * 1024 * 1024),
        name="assemble_rows",
    )(*pieces).reshape(-1, width)


def reduce_start(make_piece):
    return [flip(make_piece(j).astype(jnp.bfloat16), "dp", 1) for j in (3, 1)]


def reduce_turn(make_piece, got):
    far = make_piece(2) + got[0].astype(jnp.float32)
    return flip(far.astype(jnp.bfloat16), "dp", 2), make_piece(0) + got[1].astype(jnp.float32)


def plane_device(
    tokens,
    cotangent,
    rope_positions,
    block_order,
    w_query,
    key_weight,
    value_weight,
    w_out,
    w_gate,
    w_up,
    w_down,
    attn_gain,
    mlp_gain,
):
    f32, b16 = jnp.float32, jnp.bfloat16
    rows, width = tokens.shape[1:]
    block_size = rows // 2
    ctx_count = lax.axis_size("ctx")
    shards = lax.axis_size("fsdp")
    planes = lax.axis_size("dp")
    ctx_rank = lax.axis_index("ctx")
    shard = lax.axis_index("fsdp")
    plane = lax.axis_index("dp")
    heads = QUERY_HEADS // (shards * ctx_count)
    packed = heads * HEAD_SIZE
    lanes = -(-HEAD_SIZE // 128) * 128
    seq_rows = ctx_count * rows

    gains = gather_rows(jnp.stack([attn_gain, mlp_gain]))
    gains = jnp.stack(gains)
    gains = jnp.concatenate(
        [lax.dynamic_index_in_dim(gains, shard ^ j, 0, keepdims=False) for j in range(shards)],
        axis=1,
    ).astype(f32)
    first_gain, second_gain = gains[0], gains[1]
    pos = jnp.stack([rope_positions, flip(rope_positions, "ctx", 1)], axis=1)

    def halves(value):
        return value.reshape(2, rows // 2, width)

    x_pieces, source = gather_plane(halves(tokens[0]))

    def columns(weight, relative):
        size = weight.shape[1] // (shards * ctx_count)
        start = ((shard ^ relative) * ctx_count + ctx_rank) * size
        return lax.dynamic_slice_in_dim(weight, start, size, 1)

    def column_block(weights, k):
        return jnp.concatenate([columns(w, k) for w in weights], axis=1)

    w_rows = w_query.shape[0]
    qkv_parts = [column_block((w_query, key_weight, value_weight), k) for k in range(shards)]
    qkv_parts = [qkv_parts[0]] + [flip(qkv_parts[k], "fsdp", k) for k in range(1, shards)]
    qkv_weight = place(
        qkv_parts,
        [lambda f, z, k=k: (f ^ k) * w_rows for k in range(shards)],
        shards * w_rows,
        shard,
        plane,
    )
    gate_late, up_late, out_late = (after(w, x_pieces[1], x_pieces[2]) for w in (w_gate, w_up, w_out))
    out_rows = w_out.shape[0] // ctx_count
    own_out = lax.dynamic_slice_in_dim(w_out, ctx_rank * out_rows, out_rows, 0)
    out_blocks = out_late.reshape(ctx_count, out_rows, width)
    out_blocks = jnp.where(ctx_rank == 0, out_blocks, out_blocks[::-1])
    half_plane = plane % 2
    out_y = flip(lax.dynamic_index_in_dim(out_blocks, half_plane, 0, keepdims=False), "fsdp", 2)
    out_z = flip(out_y, "dp", 1)
    out_blocks = out_blocks.reshape(-1, width)
    out_weight = place(
        [out_blocks, flip(out_blocks, "fsdp", 1), out_y, out_z]
        + [flip(out_y, "fsdp", 1), flip(out_z, "fsdp", 1)],
        [
            lambda f, z: 0 * f,
            lambda f, z: 0 * f + ctx_count * out_rows,
            lambda f, z: (2 * ctx_count + z % 2) * out_rows,
            lambda f, z: (2 * ctx_count + 1 - z % 2) * out_rows,
            lambda f, z: (3 * ctx_count + z % 2) * out_rows,
            lambda f, z: (3 * ctx_count + 1 - z % 2) * out_rows,
        ],
        shards * ctx_count * out_rows,
        shard,
        plane,
    )
    glu_near = [column_block((gate_late, up_late), k) for k in range(2)]
    half_rows = w_rows // 2
    half_gate, half_up = (
        lax.dynamic_slice_in_dim(w, half_plane * half_rows, half_rows, 0)
        for w in (gate_late, up_late)
    )
    glu_y = [flip(column_block((half_gate, half_up), k), "fsdp", k) for k in (2, 3)]
    glu_z = [flip(value, "dp", 1) for value in glu_y]
    glu_weight = place(
        [glu_near[0], flip(glu_near[1], "fsdp", 1)] + glu_y + glu_z,
        [lambda f, z, k=k: (f ^ k) * w_rows for k in range(2)]
        + [lambda f, z, k=k: (f ^ k) * w_rows + z % 2 * half_rows for k in (2, 3)]
        + [lambda f, z, k=k: (f ^ k) * w_rows + (1 - z % 2) * half_rows for k in (2, 3)],
        shards * w_rows,
        shard,
        plane,
    )
    c_pieces, unused = gather_plane(after(halves(cotangent[0]), glu_y[0], out_y))
    cot_all = assemble(c_pieces, source, (shards, ctx_count, rows, width))
    down_rows = w_down.shape[0] // ctx_count
    own_down = lax.dynamic_slice_in_dim(w_down, ctx_rank * down_rows, down_rows, 0)
    padded_out = jnp.pad(
        own_out.reshape(heads, HEAD_SIZE, width), ((0, 0), (0, lanes - HEAD_SIZE), (0, 0))
    ).reshape(heads * lanes, width)

    pos = jnp.stack(
        [lax.dynamic_index_in_dim(pos, shard ^ j, 0, keepdims=False) for j in range(shards)]
    )
    cosine_table, sine_table = rope_tables(pos.reshape(-1))
    filler = jnp.zeros((cosine_table.shape[0], lanes - HEAD_SIZE), f32)
    cosine = jnp.concatenate([cosine_table, cosine_table, filler], axis=1)
    sine = jnp.concatenate([-sine_table, sine_table, filler], axis=1)
    own_ids = jnp.arange(rows, dtype=jnp.int32)
    seq_tokens = jnp.concatenate(
        [
            token_lookup(block_order, (ctx_rank ^ k) * rows + own_ids, block_size, rows)
            for k in range(ctx_count)
        ]
    )
    ids_row, ids_column = seq_tokens[None, :], seq_tokens[:, None]

    shape = (shards, ctx_count, rows, width, heads)
    x_all, normed_first, qkv, att = attention_forward(
        x_pieces, source, first_gain[None], qkv_weight, cosine, sine, ids_row, ids_column, shape
    )
    a_pieces, unused = gather_plane(att)
    (hidden, normed_second, grad_glu, activated, second_part, keep, send, mlp_keep, mlp_send) = (
        feed_forward(
            x_all,
            a_pieces,
            source,
            out_weight,
            second_gain[None],
            glu_weight,
            own_down,
            cot_all,
            (shards, ctx_count, rows, width, packed),
        )
    )
    ff_width = activated.shape[1]
    piece = width // planes

    def column_piece(values, j):
        return lax.dynamic_slice_in_dim(values, (plane ^ j) * piece, piece, 1)

    glu_got = reduce_start(lambda j: tn_dot(column_piece(normed_second, j), grad_glu))
    down_got = reduce_start(lambda j: tn_dot(activated, column_piece(cot_all, j)))

    grad_normed = scatter_plane(keep, send)
    own_unit2, own_root2 = normalize(hidden)
    grad_hidden, unused = norm_back(grad_normed, own_unit2, own_root2, second_gain)
    grad_hidden = grad_hidden + cotangent[0].astype(f32)
    grad_hidden_b = grad_hidden.astype(b16)
    h_pieces, unused = gather_plane(halves(grad_hidden_b))

    normed_late, cot_late = after(normed_second, grad_hidden_b), after(cot_all, grad_hidden_b)
    glu_got = [after(v, h_pieces[1]) for v in glu_got]
    down_got = [after(v, h_pieces[1]) for v in down_got]
    glu_far, glu_piece = reduce_turn(
        lambda j: tn_dot(column_piece(normed_late, j), grad_glu), glu_got
    )
    down_far, down_piece = reduce_turn(
        lambda j: tn_dot(activated, column_piece(cot_late, j)), down_got
    )

    h_all, attended, d_qkv, first_part, keep, send = attention_backward(
        h_pieces,
        source,
        padded_out,
        qkv_weight,
        qkv,
        x_all,
        cosine,
        sine,
        ids_row,
        ids_column,
        shape,
    )
    out_make = lambda j: tn_dot(attended, column_piece(h_all, j))
    qkv_make = lambda j: tn_dot(column_piece(normed_first, j), d_qkv)
    out_got = reduce_start(out_make)
    qkv_got = reduce_start(qkv_make)
    grad_normed_first = scatter_plane(keep, send)
    own_unit1, own_root1 = normalize(tokens[0].astype(f32))
    grad_input, unused = norm_back(grad_normed_first, own_unit1, own_root1, first_gain)
    grad_input = (grad_hidden + grad_input).astype(b16)
    out_far, out_piece = reduce_turn(out_make, out_got)
    qkv_far, qkv_piece = reduce_turn(qkv_make, qkv_got)
    mlp_send = after(mlp_send, h_pieces[3], h_pieces[4])
    mlp_term = scatter_plane(mlp_keep, mlp_send)
    output = (hidden + mlp_term).astype(b16)
    glu_piece = glu_piece + after(glu_far, send).astype(f32)
    down_piece = down_piece + after(down_far, send).astype(f32)
    out_piece = out_piece + out_far.astype(f32)
    qkv_piece = qkv_piece + qkv_far.astype(f32)

    gain_grads = jnp.concatenate([first_part, second_part], axis=0)
    for axis, bit in (("fsdp", 1), ("ctx", 1), ("dp", 1), ("fsdp", 2), ("dp", 2)):
        gain_grads = gain_grads + flip(gain_grads, axis, bit)
    gain_width = width // (planes * ctx_count * shards)
    gain_at = ((plane * ctx_count + ctx_rank) * shards + shard) * gain_width
    gain_grads = lax.dynamic_slice_in_dim(gain_grads, gain_at, gain_width, 1)

    def swap_rows(value):
        part = value.shape[0] // ctx_count
        kept = lax.dynamic_slice_in_dim(value, ctx_rank * part, part, 0)
        give = lax.dynamic_slice_in_dim(value, (1 - ctx_rank) * part, part, 0).astype(b16)
        return kept, flip(give, "ctx", 1).astype(f32)

    def pair(kept, got, axis):
        return jnp.where(
            ctx_rank == 0,
            jnp.concatenate([kept, got], axis=axis),
            jnp.concatenate([got, kept], axis=axis),
        )

    def swap_columns(value):
        part = value.shape[1] // ctx_count
        kept = lax.dynamic_slice_in_dim(value, ctx_rank * part, part, 1)
        give = lax.dynamic_slice_in_dim(value, (1 - ctx_rank) * part, part, 1).astype(b16)
        return pair(kept, flip(give, "ctx", 1).astype(f32), 0)

    glu_keep, glu_got = swap_rows(glu_piece)
    qkv_keep, qkv_got = swap_rows(qkv_piece)
    cuts = (0, packed, packed + HEAD_SIZE, packed + 2 * HEAD_SIZE)
    qkv_grads = [
        pair(qkv_keep[:, a:b], qkv_got[:, a:b], 1) for a, b in zip(cuts[:-1], cuts[1:])
    ]
    return (
        output[None],
        grad_input[None],
        qkv_grads[0],
        qkv_grads[1],
        qkv_grads[2],
        swap_columns(out_piece),
        pair(glu_keep[:, :ff_width], glu_got[:, :ff_width], 1),
        pair(glu_keep[:, ff_width:], glu_got[:, ff_width:], 1),
        swap_columns(down_piece),
        gain_grads[0],
        gain_grads[1],
    )


def plane_fits(mesh):
    sizes = mesh.shape
    return (
        sizes["ctx"] == 2
        and sizes["fsdp"] == 4
        and sizes["dp"] == 4
        and KEY_VALUE_HEADS == sizes["ctx"] * sizes["fsdp"]
    )


def solution(mesh):
    placed = (
        P(("dp", "fsdp"), "ctx", None),
        P(("dp", "fsdp"), "ctx", None),
        P("dp", "ctx"),
        P(),
        P("fsdp", None),
        P("fsdp", None),
        P("fsdp", None),
        P("fsdp", None),
        P("fsdp", None),
        P("fsdp", None),
        P("fsdp", None),
        P("fsdp"),
        P("fsdp"),
    )
    return jax.shard_map(
        plane_device if plane_fits(mesh) else per_device,
        mesh=mesh,
        in_specs=placed,
        out_specs=(
            P(("dp", "fsdp"), "ctx", None),
            P(("dp", "fsdp"), "ctx", None),
            P(("dp", "ctx"), "fsdp"),
            P(("dp", "ctx"), "fsdp"),
            P(("dp", "ctx"), "fsdp"),
            P("fsdp", ("dp", "ctx")),
            P(("dp", "ctx"), "fsdp"),
            P(("dp", "ctx"), "fsdp"),
            P("fsdp", ("dp", "ctx")),
            P(("dp", "ctx", "fsdp")),
            P(("dp", "ctx", "fsdp")),
        ),
        check_vma=False,
    )
```
